32 devices in a mesh: dp: 4 (over y, x), concept: 8 (over z, core).
Axes of the slice: x: 2, y: 2, z: 4, core: 2. Of those that a mesh axis runs over, the one named last changes fastest.
Arguments:
- embeddings: bfloat16 [32768, 1024], P(('dp', 'concept')), may hold values from -720 to 720
- row_weight: bfloat16 [32768], P(('dp', 'concept')), may hold values from 0.25 to 4
- group_label: int32 [32768, 1], P(('dp', 'concept')), may hold values from 0 to 7; in each aligned block of 1024 rows (0 to 1023, 1024 to 2047, ...) at most 256 rows name the same one
- concept_label: int32 [32768], P(('dp', 'concept')), may hold values from 0 to 1023
- level1_weight: bfloat16 [1024, 8], replicated, may hold values from -0.1875 to 0.1875
- level2_weight: bfloat16 [8, 1024, 1024], P('concept'), may hold values from -0.1875 to 0.1875
Outputs:
- row_loss: float32 [32768], P(('dp', 'concept'))
- embed_grad: bfloat16 [32768, 1024], P(('dp', 'concept'))
- level1_grad: float32 [1024, 8], replicated
- level2_grad: bfloat16 [8, 1024, 1024], P('concept', 'dp')
The draws below stay inside these ranges and needn't reach their ends.
Inputs may be any that keep to these rules, and one draw needn't show every extreme that they name: `group_label`: among the rows of one device, no group is named more than 256 times, a bound that some block reaches.
All inputs are finite; a program needn't handle non-finite values.
Results may differ from the reference program's by a relative error of at most 0.0051.
Values may be sent and summed in bfloat16 or wider, within the bound.
No kernel may reach another device: no remote copies, remote signals or barrier semaphores. Data moves between devices by JAX's collectives and lax.ppermute only.
A program may use at most 128 MiB of HBM per device.

```python
import math
import jax
import jax.numpy as jnp
import numpy as np
from jax import lax

D = 1024
C = 1024
ROW_DEV = 1024
GROUPS = 8
CAP = 256
ROWS = 32768


def draw_embeddings(key, part):
    first = jax.random.fold_in(key, 0)
    base = jnp.clip(jax.random.normal(first, (ROWS, D), jnp.float32), -6.0, 6.0)
    return base.astype(jnp.bfloat16)


def place_ends(entries, own_key, smallest, top_value):
    extent = entries.shape
    index_at = [jax.random.randint(jax.random.fold_in(own_key, axis), (), 0, extent[axis]) for axis in range(len(extent))]
    entries = entries.at[tuple(index_at)].set(smallest)
    longest = extent.index(max(extent))
    index_at[longest] = (index_at[longest] + 1) % extent[longest]
    return entries.at[tuple(index_at)].set(top_value)


def shard_levels(rng, extent, pieces, low, top_value):
    def one(position, blocks):
        steps = jax.random.uniform(jax.random.fold_in(jax.random.fold_in(rng, 6), position), (blocks,), jnp.float32, low / len(pieces), top_value / len(pieces))
        return jnp.repeat(jnp.exp(steps), extent[position] // blocks).reshape((-1,) + (1,) * (len(extent) - position - 1))

    level = one(*pieces[0])
    for cut in pieces[1:]:
        level = level * one(*cut)
    return level


def shared_out(key, own, number, rows, count, top, bound, skew):
    sequence = jax.random.permutation(key, count)
    crowded, ordinary = shares(count, rows * top, bound, skew, True), shares(count, rows * top, bound, skew, False)
    places = jnp.arange(count)

    def named(lengths, turn):
        used = int((lengths > 0).sum())
        fixed = max(1, used // 4)
        passed = fixed + (places - fixed + turn * (used - fixed)) % max(1, count - fixed)
        return jnp.zeros((count,), jnp.int32).at[sequence[jnp.where(places < fixed, places, passed)]].set(jnp.asarray(lengths, jnp.int32))

    lengths = jnp.where(number % 4 == 0, named(crowded, number // 4), named(ordinary, number - number // 4 - 1))
    mixed = jax.random.permutation(jax.random.fold_in(own, 3), count)
    giver, taker = mixed[0:count // 2 * 2:2], mixed[1:count // 2 * 2:2]
    margin = jnp.minimum(lengths[giver] - 1, bound - lengths[taker]) // 2
    margin = jnp.where((giver == sequence[0]) | (taker == sequence[0]) | (lengths[taker] == 0), 0, jnp.maximum(margin, 0))
    passed = jax.random.randint(jax.random.fold_in(own, 4), (count // 2,), 0, 1 << 20) % (margin + 1)
    lengths = lengths.at[giver].add(-passed).at[taker].add(passed)
    items = jnp.searchsorted(jnp.cumsum(lengths), jnp.arange(rows * top), side="right").astype(jnp.int32)
    grid = items.reshape(top, rows).T
    grid = grid[jax.random.permutation(jax.random.fold_in(own, 1), rows)]
    turn = jax.random.randint(jax.random.fold_in(own, 2), (rows, 1), 0, top)
    return jnp.take_along_axis(grid, (jnp.arange(top)[None, :] + turn) % top, axis=1)


def shares(amount, total, limit, slope, full):
    weights = [(1 << 20) // math.isqrt(standing ** slope) + 1 for standing in range(1, amount + 1)]
    largest = limit if full else min(limit, max(-(-total // amount), total * weights[0] // sum(weights)))
    least = 1 if total - largest >= amount - 1 else 0
    given, rest = [largest] + [least] * (amount - 1), total - largest - least * (amount - 1)
    while rest > 0:
        free = [i for i in range(1, amount) if given[i] < largest] or [i for i in range(1, amount) if given[i] < limit]
        mass, budget = sum([weights[i] for i in free]), rest
        for i in free:
            addition = min(limit - given[i], max(1, budget * weights[i] // mass), rest)
            given[i] = given[i] + addition
            rest = rest - addition
    return np.array(given)


def noise(key, dims, width, reach, cuts=(), held_as=jnp.bfloat16):
    factor_of = shard_levels(key, dims, cuts, -0.22, 0.18) if cuts else 1.0
    result = jax.random.normal(key, dims, jnp.float32) * width * factor_of
    return jnp.minimum(jnp.maximum(result, -reach), reach).astype(held_as)


def setup_inputs(seed: int = 0) -> dict:
    splits = jax.random.split(jax.random.key(seed), 7)
    embeddings = draw_embeddings(jax.random.fold_in(splits[6], 71), 0)
    row_weight = jnp.clip(jnp.exp(math.log(4.0) - 2.7725887 * jax.random.uniform(splits[1], (ROWS,), jnp.float32) ** shard_levels(splits[1], (ROWS,), ((0, 32),), -0.2, 0.2)), 0.25, 4.0).astype(jnp.bfloat16)
    group_label_keys = jax.random.split(jax.random.fold_in(splits[2], 1), ROWS // ROW_DEV)
    group_label_turns = jax.random.permutation(jax.random.fold_in(splits[2], 3), ROWS // ROW_DEV)
    group_label = jax.vmap(lambda own, number: shared_out(jax.random.fold_in(splits[2], 2), own, number, ROW_DEV, GROUPS, 1, CAP, 2))(group_label_keys, group_label_turns).reshape((ROWS, 1))
    concept_label = place_ends(jax.random.randint(splits[3], (ROWS,), 0, C), jax.random.fold_in(splits[3], 1), 0, C - 1).astype(jnp.int32)
    level1_weight = noise(splits[4], (D, GROUPS), D ** -0.5, 0.1875)
    level2_weight = noise(splits[5], (GROUPS, D, C), D ** -0.5, 0.1875, ((0, 8),))
    return dict(embeddings=embeddings, row_weight=row_weight, group_label=group_label, concept_label=concept_label, level1_weight=level1_weight, level2_weight=level2_weight)


def reference(embeddings, row_weight, group_label, concept_label, level1_weight, level2_weight):
    groups = group_label[:, 0].astype(jnp.int32)
    weights = row_weight.astype(jnp.float32)
    z1 = jnp.dot(embeddings, level1_weight, preferred_element_type=jnp.float32)
    top1 = jnp.max(z1, axis=1, keepdims=True)
    exps1 = jnp.exp(z1 - top1)
    total1 = jnp.sum(exps1, axis=1, keepdims=True)
    probs1 = exps1 / total1
    onehot1 = (groups[:, None] == jnp.arange(GROUPS, dtype=jnp.int32)[None, :]).astype(jnp.float32)
    loss1 = top1[:, 0] + jnp.log(total1[:, 0]) - jnp.sum(z1 * onehot1, axis=1)
    dz1 = (weights[:, None] * (probs1 - onehot1)).astype(jnp.bfloat16)
    level1_grad = lax.dot_general(embeddings, dz1, (((0,), (0,)), ((), ())), preferred_element_type=jnp.float32)
    dx1 = jnp.dot(dz1, level1_weight.T, preferred_element_type=jnp.float32)

    gmax = 2 * ROWS // GROUPS
    counts = jnp.sum(onehot1, axis=0).astype(jnp.int32)
    order = jnp.argsort(groups, stable=True).astype(jnp.int32)
    starts = (jnp.cumsum(counts) - counts).astype(jnp.int32)
    slots = jnp.arange(gmax, dtype=jnp.int32)
    table = starts[:, None] + slots[None, :]
    valid = slots[None, :] < counts[:, None]
    row_index = order[jnp.minimum(table, ROWS - 1)]
    row_index = jnp.where(valid, row_index, ROWS).astype(jnp.int32)

    def one_group(carry, inputs):
        grad_all, loss_all = carry
        index, weight = inputs
        safe = jnp.minimum(index, ROWS - 1)
        rows = embeddings[safe]
        labels = concept_label[safe]
        scale = jnp.where(index < ROWS, weights[safe], 0.0)
        z2 = jnp.dot(rows, weight, preferred_element_type=jnp.float32)
        top2 = jnp.max(z2, axis=1, keepdims=True)
        exps2 = jnp.exp(z2 - top2)
        total2 = jnp.sum(exps2, axis=1, keepdims=True)
        probs2 = exps2 / total2
        onehot2 = (labels[:, None] == jnp.arange(C, dtype=jnp.int32)[None, :]).astype(jnp.float32)
        loss2 = (top2[:, 0] + jnp.log(total2[:, 0]) - jnp.sum(z2 * onehot2, axis=1)).astype(jnp.bfloat16)
        dz2 = (scale[:, None] * (probs2 - onehot2)).astype(jnp.bfloat16)
        dx2 = jnp.dot(dz2, weight.T, preferred_element_type=jnp.float32).astype(jnp.bfloat16)
        grad_w = lax.dot_general(rows, dz2, (((0,), (0,)), ((), ())), preferred_element_type=jnp.float32)
        grad_all = grad_all.at[index].set(dx2, mode="drop")
        loss_all = loss_all.at[index].set(loss2.astype(jnp.float32), mode="drop")
        return (grad_all, loss_all), grad_w.astype(jnp.bfloat16)

    start = (jnp.zeros((ROWS, D), jnp.bfloat16), jnp.zeros((ROWS,), jnp.float32))
    (dx2_all, loss2_all), level2_grad = lax.scan(one_group, start, (row_index, level2_weight))
    embed_grad = (dx1 + dx2_all.astype(jnp.float32)).astype(jnp.bfloat16)
    row_loss = loss1 + loss2_all
    return row_loss, embed_grad, level1_grad, level2_grad
```

```python
import jax
import jax.numpy as jnp
from jax import lax
from jax.experimental import pallas as pl
from jax.experimental.pallas import tpu as pltpu
from jax.sharding import PartitionSpec as P

LANES = 128
F32, BF16 = jnp.float32, jnp.bfloat16
AXES = ("dp", "concept")


def first_level(embeddings, weights, groups, level1_weight):
    groups_n = level1_weight.shape[1]
    z1 = jnp.dot(embeddings, level1_weight, preferred_element_type=jnp.float32)
    top1 = jnp.max(z1, axis=1, keepdims=True)
    exps1 = jnp.exp(z1 - top1)
    total1 = jnp.sum(exps1, axis=1, keepdims=True)
    probs1 = exps1 / total1
    onehot1 = (groups[:, None] == jnp.arange(groups_n, dtype=jnp.int32)[None, :]).astype(
        jnp.float32
    )
    loss1 = top1[:, 0] + jnp.log(total1[:, 0]) - jnp.sum(z1 * onehot1, axis=1)
    dz1 = (weights[:, None] * (probs1 - onehot1)).astype(jnp.bfloat16)
    partial_grad = lax.dot_general(
        embeddings, dz1, (((0,), (0,)), ((), ())), preferred_element_type=jnp.float32
    )
    dx1 = jnp.dot(dz1, level1_weight.T, preferred_element_type=jnp.float32)
    level1_grad = lax.psum(partial_grad, ("dp", "concept"))
    return (loss1, dx1, level1_grad)


def on_device(embeddings, row_weight, group_label, concept_label, level1_weight, level2_weight):
    rows_n, width = embeddings.shape
    groups_n = level1_weight.shape[1]
    concepts = level2_weight.shape[2]
    capacity = 2 * rows_n // groups_n
    groups = group_label[:, 0]
    weights = row_weight.astype(jnp.float32)
    member = (groups[:, None] == jnp.arange(groups_n, dtype=jnp.int32)[None, :]).astype(
        jnp.bfloat16
    )
    positions = jnp.arange(rows_n, dtype=jnp.int32)
    earlier = (positions[None, :] < positions[:, None]).astype(jnp.bfloat16)
    before = jnp.dot(earlier, member, preferred_element_type=jnp.float32)
    rank = jnp.sum(before * member.astype(jnp.float32), axis=1).astype(jnp.int32)
    slot = groups * capacity + rank
    source = jnp.full((groups_n * capacity,), rows_n, jnp.int32).at[slot].set(positions)
    filled = source < rows_n
    safe = jnp.minimum(source, rows_n - 1)
    send_rows = jnp.where(filled[:, None], embeddings[safe], jnp.zeros((), jnp.bfloat16)).reshape(
        groups_n, capacity, width
    )
    send_weight = jnp.where(filled, row_weight[safe], jnp.zeros((), jnp.bfloat16)).reshape(
        groups_n, capacity
    )
    send_label = jnp.where(filled, concept_label[safe], 0).reshape(groups_n, capacity)
    loss1, dx1, level1_grad = first_level(embeddings, weights, groups, level1_weight)
    recv_rows, recv_weight, recv_label = (
        lax.all_to_all(send_rows, "concept", split_axis=0, concat_axis=1, tiled=True),
        lax.all_to_all(send_weight, "concept", split_axis=0, concat_axis=1, tiled=True),
        lax.all_to_all(send_label, "concept", split_axis=0, concat_axis=1, tiled=True),
    )
    z2 = jnp.einsum("grd,gdc->grc", recv_rows, level2_weight, preferred_element_type=jnp.float32)
    top2 = jnp.max(z2, axis=2, keepdims=True)
    exps2 = jnp.exp(z2 - top2)
    total2 = jnp.sum(exps2, axis=2, keepdims=True)
    probs2 = exps2 / total2
    onehot2 = (
        recv_label[:, :, None] == jnp.arange(concepts, dtype=jnp.int32)[None, None, :]
    ).astype(jnp.float32)
    loss2 = (top2[:, :, 0] + jnp.log(total2[:, :, 0]) - jnp.sum(z2 * onehot2, axis=2)).astype(
        jnp.bfloat16
    )
    dz2 = (recv_weight.astype(jnp.float32)[:, :, None] * (probs2 - onehot2)).astype(jnp.bfloat16)
    dx2 = jnp.einsum("grc,gdc->grd", dz2, level2_weight, preferred_element_type=jnp.float32).astype(
        jnp.bfloat16
    )
    back_grad, back_loss = (
        lax.all_to_all(dx2, "concept", split_axis=1, concat_axis=0, tiled=True),
        lax.all_to_all(loss2, "concept", split_axis=1, concat_axis=0, tiled=True),
    )
    summed = lax.psum_scatter(
        jnp.einsum("grd,grc->dgc", recv_rows, dz2, preferred_element_type=jnp.float32),
        "dp",
        scatter_dimension=0,
        tiled=True,
    )
    level2_grad = jnp.transpose(summed, (1, 0, 2)).astype(jnp.bfloat16)
    dx2_rows = back_grad.reshape(groups_n * capacity, width)[slot]
    loss2_rows = back_loss.reshape(groups_n * capacity)[slot]
    embed_grad = (dx1 + dx2_rows.astype(jnp.float32)).astype(jnp.bfloat16)
    row_loss = loss1 + loss2_rows.astype(jnp.float32)
    return (row_loss, embed_grad, level1_grad, level2_grad)


def nn(a, b):
    return lax.dot_general(a, b, (((1,), (0,)), ((), ())), preferred_element_type=F32)


def nt(a, b):
    return lax.dot_general(a, b, (((1,), (1,)), ((), ())), preferred_element_type=F32)


def tn(a, b):
    return lax.dot_general(a, b, (((0,), (0,)), ((), ())), preferred_element_type=F32)


def dispatch_kernel(key_ref, aux_ref, rows_ref, theirs_ref, mine_ref):
    s = pl.program_id(0)
    cap = mine_ref.shape[0]
    rows_n, width = rows_ref.shape
    place = lax.broadcasted_iota(jnp.int32, (cap, rows_n), 0)
    for out_ref, t in ((theirs_ref, 2 * s + 1), (mine_ref, 2 * s)):
        pick = (key_ref[...] == place + t * cap).astype(F32).astype(BF16)
        out_ref[:, :width] = nn(pick, rows_ref[...]).astype(BF16)
        out_ref[:, width:] = nt(pick, aux_ref[...]).astype(BF16)


def dispatch(key, aux, rows, groups_n, cap):
    rows_n, width = rows.shape
    full = width + LANES
    half = groups_n // 2
    out = jax.ShapeDtypeStruct((half, cap, full), BF16)
    block = pl.BlockSpec((pl.Squeezed(), cap, full), lambda s: (s, 0, 0))
    return pl.pallas_call(
        dispatch_kernel,
        grid=(half,),
        in_specs=[
            pl.BlockSpec((1, rows_n), lambda s: (0, 0)),
            pl.BlockSpec((LANES, rows_n), lambda s: (0, 0)),
            pl.BlockSpec((rows_n, width), lambda s: (0, 0)),
        ],
        out_specs=[block, block],
        out_shape=[out, out],
        compiler_params=pltpu.CompilerParams(vmem_limit_bytes=24 << 20),
        cost_estimate=pl.CostEstimate(
            flops=2 * groups_n * cap * rows_n * full,
            bytes_accessed=2 * (rows_n * width + groups_n * cap * full),
            transcendentals=0,
        ),
        name="dispatch",
    )(key, aux, rows)


def group_kernel(n_blocks, n_pieces, sizes, meta_ref, *refs):
    blocks, refs = refs[:n_blocks], refs[n_blocks:]
    pieces, refs = refs[:n_pieces], refs[n_pieces:]
    outs, refs = refs[:n_blocks], refs[n_blocks:]
    to_x, to_y, keep_a, keep_b, x_s, w_s, dz_s, dx_s, g_s, sems = refs
    width, concepts = w_s.shape
    cap = sizes[0]
    total = x_s.shape[0]
    copies = []
    for i, piece in enumerate(pieces):
        start = pl.multiple_of(meta_ref[i], LANES)
        copies.append(
            pltpu.make_async_copy(piece, w_s.at[pl.ds(start, piece.shape[0])], sems.at[i])
        )
    at = 0
    for i, block in enumerate(blocks):
        copies.append(
            pltpu.make_async_copy(block, x_s.at[pl.ds(at, block.shape[0])], sems.at[n_pieces + i])
        )
        at += block.shape[0]
    for copy in copies:
        copy.start()
    for copy in copies:
        copy.wait()
    column = lax.broadcasted_iota(jnp.int32, (cap, concepts), 1)

    @pl.loop(0, total // cap)
    def _(b):
        here = pl.ds(pl.multiple_of(b * cap, cap), cap)
        z = nn(x_s[here, :width], w_s[...])
        aux = x_s[here, width:].astype(F32)
        weight = aux[:, 0:1]
        label = (aux[:, 1:2] * 32.0 + aux[:, 2:3]).astype(jnp.int32)
        hot = column == label
        top = jnp.max(z, axis=1, keepdims=True)
        exps = jnp.exp(z - top)
        mass = jnp.sum(exps, axis=1, keepdims=True)
        picked = jnp.sum(jnp.where(hot, z, 0.0), axis=1, keepdims=True)
        probs = exps * (1.0 / mass)
        dz = (weight * (probs - jnp.where(hot, 1.0, 0.0))).astype(BF16)
        dz_s[here, :] = dz
        dx_s[here, :width] = nt(dz, w_s[...]).astype(BF16)
        loss = top + jnp.log(mass) - picked
        dx_s[here, width:] = jnp.broadcast_to(loss, (cap, LANES)).astype(BF16)

    copies = []
    at = 0
    for i, out in enumerate(outs):
        copies.append(
            pltpu.make_async_copy(dx_s.at[pl.ds(at, out.shape[0])], out, sems.at[i])
        )
        copies[-1].start()
        at += out.shape[0]
    quarter, part = g_s.shape[1], g_s.shape[2]

    for j in range(8):
        start = pl.multiple_of(meta_ref[n_pieces + j], LANES)
        half = (0, 0, 1, 1, 0, 0, 1, 1)[j]
        g_s[j] = tn(
            x_s[:, pl.ds(start, quarter)], dz_s[:, half * part : (half + 1) * part]
        ).astype(BF16)
        if j % 2 == 1:
            out = (to_x, to_y, keep_a, keep_b)[j // 2]
            copies.append(
                pltpu.make_async_copy(g_s.at[pl.ds(j - 1, 2)], out, sems.at[n_blocks + j // 2])
            )
            copies[-1].start()
    for copy in copies:
        copy.wait()


def group_step(blocks, pieces, starts, quarters, concepts, cap, name):
    full = blocks[0].shape[1]
    width = full - LANES
    total = sum(b.shape[0] for b in blocks)
    quarter, part = width // 4, concepts // 2
    meta = jnp.stack(starts + [q * quarter for q in quarters]).astype(jnp.int32)
    any_spec = pl.BlockSpec(memory_space=pl.ANY)
    grad = jax.ShapeDtypeStruct((2, quarter, part), BF16)
    n_sems = max(len(pieces) + len(blocks), len(blocks) + 4)
    res = pl.pallas_call(
        lambda *refs: group_kernel(len(blocks), len(pieces), (cap,), *refs),
        in_specs=[pl.BlockSpec(memory_space=pltpu.SMEM)] + [any_spec] * (len(blocks) + len(pieces)),
        out_specs=[any_spec] * (len(blocks) + 4),
        out_shape=[jax.ShapeDtypeStruct(b.shape, BF16) for b in blocks] + [grad] * 4,
        scratch_shapes=[
            pltpu.VMEM((total, full), BF16),
            pltpu.VMEM((width, concepts), BF16),
            pltpu.VMEM((total, concepts), BF16),
            pltpu.VMEM((total, full), BF16),
            pltpu.VMEM((8, quarter, part), BF16),
            pltpu.SemaphoreType.DMA((n_sems,)),
        ],
        compiler_params=pltpu.CompilerParams(vmem_limit_bytes=32 << 20),
        cost_estimate=pl.CostEstimate(
            flops=6 * total * width * concepts,
            bytes_accessed=4 * (total * full + width * concepts),
            transcendentals=total * concepts,
        ),
        name=name,
    )(meta, *blocks, *pieces)
    return res[: len(blocks)], res[len(blocks) :]


def combine_kernel(n_blocks, cap, key_ref, loss_ref, dz1_ref, w1_ref, *refs):
    blocks, refs = refs[:n_blocks], refs[n_blocks:]
    out_ref, row_loss_ref, x_s, sems = refs

    @pl.when(pl.program_id(0) == 0)
    def _():
        copies = [
            pltpu.make_async_copy(b, x_s.at[pl.ds(i * cap, cap)], sems.at[i])
            for i, b in enumerate(blocks)
        ]
        for copy in copies:
            copy.start()
        for copy in copies:
            copy.wait()

    tile, width = out_ref.shape
    slots = x_s.shape[0]
    place = lax.broadcasted_iota(jnp.int32, (tile, slots), 1)
    pick = (key_ref[...] == place).astype(F32).astype(BF16)
    got = nn(pick, x_s[...])
    dx1 = nt(dz1_ref[...], w1_ref[...])
    out_ref[...] = (dx1 + got[:, :width]).astype(BF16)
    row_loss_ref[...] = loss_ref[...] + got[:, width : width + 1]


def combine(key, loss1, dz1, w1, blocks, cap):
    rows_n = key.shape[0]
    width = w1.shape[0]
    full = width + LANES
    tile = cap
    slots = cap * len(blocks)
    return pl.pallas_call(
        lambda *refs: combine_kernel(len(blocks), cap, *refs),
        grid=(rows_n // tile,),
        in_specs=[
            pl.BlockSpec((tile, 1), lambda i: (i, 0)),
            pl.BlockSpec((tile, 1), lambda i: (i, 0)),
            pl.BlockSpec((tile, LANES), lambda i: (i, 0)),
            pl.BlockSpec((width, LANES), lambda i: (0, 0)),
        ]
        + [pl.BlockSpec(memory_space=pl.ANY)] * len(blocks),
        out_specs=[
            pl.BlockSpec((tile, width), lambda i: (i, 0)),
            pl.BlockSpec((tile, 1), lambda i: (i, 0)),
        ],
        out_shape=[
            jax.ShapeDtypeStruct((rows_n, width), BF16),
            jax.ShapeDtypeStruct((rows_n, 1), F32),
        ],
        scratch_shapes=[
            pltpu.VMEM((slots, full), BF16),
            pltpu.SemaphoreType.DMA((len(blocks),)),
        ],
        compiler_params=pltpu.CompilerParams(vmem_limit_bytes=24 << 20),
        cost_estimate=pl.CostEstimate(
            flops=2 * rows_n * slots * full,
            bytes_accessed=2 * (slots * full + rows_n * width),
            transcendentals=0,
        ),
        name="combine",
    )(key, loss1, dz1, w1, *blocks)


def make_local(dp_n, concept_n):
    def pairs(dp_bit, concept_bit):
        return [
            (d * concept_n + c, (d ^ dp_bit) * concept_n + (c ^ concept_bit))
            for d in range(dp_n)
            for c in range(concept_n)
        ]

    core, near, far, side, up = (
        pairs(0, 1),
        pairs(0, 2),
        pairs(0, 4),
        pairs(1, 0),
        pairs(2, 0),
    )

    def send(a, to):
        return lax.ppermute(a, AXES, to)

    def local(embeddings, row_weight, group_label, concept_label, level1_weight, level2_weight):
        rows_n, width = embeddings.shape
        groups_n = level1_weight.shape[1]
        concepts = level2_weight.shape[2]
        cap = 2 * rows_n // groups_n
        quarter, part = width // dp_n, concepts // 2
        dp, me = lax.axis_index("dp"), lax.axis_index("concept")

        own = level2_weight[0]
        first = lax.dynamic_slice_in_dim(own, dp * quarter, quarter, 0)
        far2 = send(first, far)
        far3 = send(far2, near)

        def spread(q):
            qx, qy = send(q, side), send(q, up)
            half = quarter // 2
            return [q, qx, qy, send(qx[:half], up), send(qy[half:], side)]

        pieces2 = spread(far2)
        pieces3 = spread(far3)
        starts = [
            dp * quarter,
            (dp ^ 1) * quarter,
            (dp ^ 2) * quarter,
            (dp ^ 3) * quarter,
            (dp ^ 3) * quarter + quarter // 2,
        ]
        order = [dp ^ 1, dp ^ 3, dp ^ 2, dp ^ 3, dp, dp ^ 2, dp, dp ^ 1]

        groups = group_label[:, 0]
        kinds = lax.broadcasted_iota(jnp.int32, (groups_n, rows_n), 0)
        member = groups[None, :] == kinds
        positions = jnp.arange(rows_n, dtype=jnp.int32)
        earlier = (positions[:, None] < positions[None, :]).astype(BF16)
        before = nn(member.astype(BF16), earlier)
        rank = jnp.sum(jnp.where(member, before, 0.0), axis=0).astype(jnp.int32)
        key = (groups ^ me) * cap + rank
        kind = lax.broadcasted_iota(jnp.int32, (LANES, rows_n), 0)
        high = (concept_label >> 5).astype(BF16)
        low = (concept_label & 31).astype(BF16)
        zero = jnp.zeros((), BF16)
        aux = jnp.where(
            kind == 0,
            row_weight[None, :],
            jnp.where(
                kind == 1, high[None, :], jnp.where(kind == 2, low[None, :], zero)
            ),
        )
        theirs, mine = dispatch(key[None, :], aux, embeddings, groups_n, cap)
        got = send(theirs, core)
        rows_out = jnp.concatenate([mine[1], got[1]], axis=0)
        rows_in = send(rows_out, near)

        weights = row_weight.astype(F32)
        z1 = nn(embeddings, level1_weight)
        top1 = jnp.max(z1, axis=1, keepdims=True)
        exps1 = jnp.exp(z1 - top1)
        total1 = jnp.sum(exps1, axis=1, keepdims=True)
        onehot1 = (groups[:, None] == jnp.arange(groups_n, dtype=jnp.int32)[None, :]).astype(F32)
        loss1 = top1 + jnp.log(total1) - jnp.sum(z1 * onehot1, axis=1, keepdims=True)
        dz1 = (weights[:, None] * (exps1 / total1 - onehot1)).astype(BF16)
        grad1 = tn(dz1, embeddings)
        for to in (core, side, up, near, far):
            grad1 = grad1 + send(grad1, to)

        whole = [jnp.zeros((), jnp.int32)]
        step = lambda blocks, pieces, at, name: group_step(
            blocks, pieces, at, order, concepts, cap, name
        )
        dx_2, grads_2 = step([mine[2], got[2]], pieces2, starts, "far_two")
        dx_0, grads_0 = step([mine[0], got[0], rows_in], [own], whole, "own")
        dx_3, grads_3 = step([mine[3], got[3]], pieces3, starts, "far_three")

        def scatter(grads):
            to_x, to_y, keep_a, keep_b = (g for g in grads)
            from_x, from_y = send(to_x, side), send(to_y, up)
            pass_a = (keep_a[1].astype(F32) + from_x[1].astype(F32)).astype(BF16)
            pass_b = (keep_b[1].astype(F32) + from_y[1].astype(F32)).astype(BF16)
            last_a, last_b = send(pass_a, up), send(pass_b, side)
            sum_a = keep_a[0].astype(F32) + from_x[0].astype(F32) + last_a.astype(F32)
            sum_b = keep_b[0].astype(F32) + from_y[0].astype(F32) + last_b.astype(F32)
            return sum_a, sum_b

        a2, b2 = scatter(grads_2)
        a3, b3 = scatter(grads_3)
        a0, b0 = scatter(grads_0)
        a3, b3 = send(a3.astype(BF16), near), send(b3.astype(BF16), near)
        a2 = send((a2 + a3.astype(F32)).astype(BF16), far)
        b2 = send((b2 + b3.astype(F32)).astype(BF16), far)
        level2_grad = jnp.concatenate(
            [a0 + a2.astype(F32), b0 + b2.astype(F32)], axis=1
        ).astype(BF16)[None]

        dx_1 = send(dx_0[2], near)
        home = [
            dx_0[0],
            send(dx_0[1], core),
            dx_1[:cap],
            send(dx_1[cap:], core),
            dx_2[0],
            send(dx_2[1], core),
            dx_3[0],
            send(dx_3[1], core),
        ]
        pad = lambda a: jnp.pad(a, ((0, 0), (0, LANES - groups_n)))
        embed_grad, row_loss = combine(
            key[:, None], loss1, pad(dz1), pad(level1_weight), home, cap
        )
        return (row_loss[:, 0], embed_grad, grad1.T, level2_grad)

    return local


def solution(mesh):
    dp_n, concept_n = mesh.shape["dp"], mesh.shape["concept"]
    few = dp_n == 4 and concept_n == 8
    return jax.shard_map(
        make_local(dp_n, concept_n) if few else on_device,
        mesh=mesh,
        in_specs=(
            P(("dp", "concept"), None),
            P(("dp", "concept")),
            P(("dp", "concept"), None),
            P(("dp", "concept")),
            P(),
            P("concept", None, None),
        ),
        out_specs=(P(("dp", "concept")), P(("dp", "concept"), None), P(), P("concept", "dp", None)),
        check_vma=False,
    )
```

```python
import jax
import jax.numpy as jnp
from jax import lax
from jax.experimental import pallas as pl
from jax.experimental.pallas import tpu as pltpu
from jax.sharding import PartitionSpec as P

LANES = 128
PIECES = 2
F32, BF16 = jnp.float32, jnp.bfloat16
AXES = ("dp", "concept")


def first_level(embeddings, weights, groups, level1_weight):
    groups_n = level1_weight.shape[1]
    z1 = jnp.dot(embeddings, level1_weight, preferred_element_type=jnp.float32)
    top1 = jnp.max(z1, axis=1, keepdims=True)
    exps1 = jnp.exp(z1 - top1)
    total1 = jnp.sum(exps1, axis=1, keepdims=True)
    probs1 = exps1 / total1
    onehot1 = (groups[:, None] == jnp.arange(groups_n, dtype=jnp.int32)[None, :]).astype(
        jnp.float32
    )
    loss1 = top1[:, 0] + jnp.log(total1[:, 0]) - jnp.sum(z1 * onehot1, axis=1)
    dz1 = (weights[:, None] * (probs1 - onehot1)).astype(jnp.bfloat16)
    partial_grad = lax.dot_general(
        embeddings, dz1, (((0,), (0,)), ((), ())), preferred_element_type=jnp.float32
    )
    dx1 = jnp.dot(dz1, level1_weight.T, preferred_element_type=jnp.float32)
    level1_grad = lax.psum(partial_grad, ("dp", "concept"))
    return (loss1, dx1, level1_grad)


def on_device(embeddings, row_weight, group_label, concept_label, level1_weight, level2_weight):
    rows_n, width = embeddings.shape
    groups_n = level1_weight.shape[1]
    concepts = level2_weight.shape[2]
    capacity = 2 * rows_n // groups_n
    groups = group_label[:, 0]
    weights = row_weight.astype(jnp.float32)
    member = (groups[:, None] == jnp.arange(groups_n, dtype=jnp.int32)[None, :]).astype(
        jnp.bfloat16
    )
    positions = jnp.arange(rows_n, dtype=jnp.int32)
    earlier = (positions[None, :] < positions[:, None]).astype(jnp.bfloat16)
    before = jnp.dot(earlier, member, preferred_element_type=jnp.float32)
    rank = jnp.sum(before * member.astype(jnp.float32), axis=1).astype(jnp.int32)
    slot = groups * capacity + rank
    source = jnp.full((groups_n * capacity,), rows_n, jnp.int32).at[slot].set(positions)
    filled = source < rows_n
    safe = jnp.minimum(source, rows_n - 1)
    send_rows = jnp.where(filled[:, None], embeddings[safe], jnp.zeros((), jnp.bfloat16)).reshape(
        groups_n, capacity, width
    )
    send_weight = jnp.where(filled, row_weight[safe], jnp.zeros((), jnp.bfloat16)).reshape(
        groups_n, capacity
    )
    send_label = jnp.where(filled, concept_label[safe], 0).reshape(groups_n, capacity)
    loss1, dx1, level1_grad = first_level(embeddings, weights, groups, level1_weight)
    recv_rows, recv_weight, recv_label = (
        lax.all_to_all(send_rows, "concept", split_axis=0, concat_axis=1, tiled=True),
        lax.all_to_all(send_weight, "concept", split_axis=0, concat_axis=1, tiled=True),
        lax.all_to_all(send_label, "concept", split_axis=0, concat_axis=1, tiled=True),
    )
    z2 = jnp.einsum("grd,gdc->grc", recv_rows, level2_weight, preferred_element_type=jnp.float32)
    top2 = jnp.max(z2, axis=2, keepdims=True)
    exps2 = jnp.exp(z2 - top2)
    total2 = jnp.sum(exps2, axis=2, keepdims=True)
    probs2 = exps2 / total2
    onehot2 = (
        recv_label[:, :, None] == jnp.arange(concepts, dtype=jnp.int32)[None, None, :]
    ).astype(jnp.float32)
    loss2 = (top2[:, :, 0] + jnp.log(total2[:, :, 0]) - jnp.sum(z2 * onehot2, axis=2)).astype(
        jnp.bfloat16
    )
    dz2 = (recv_weight.astype(jnp.float32)[:, :, None] * (probs2 - onehot2)).astype(jnp.bfloat16)
    dx2 = jnp.einsum("grc,gdc->grd", dz2, level2_weight, preferred_element_type=jnp.float32).astype(
        jnp.bfloat16
    )
    back_grad, back_loss = (
        lax.all_to_all(dx2, "concept", split_axis=1, concat_axis=0, tiled=True),
        lax.all_to_all(loss2, "concept", split_axis=1, concat_axis=0, tiled=True),
    )
    summed = lax.psum_scatter(
        jnp.einsum("grd,grc->dgc", recv_rows, dz2, preferred_element_type=jnp.float32),
        "dp",
        scatter_dimension=0,
        tiled=True,
    )
    level2_grad = jnp.transpose(summed, (1, 0, 2)).astype(jnp.bfloat16)
    dx2_rows = back_grad.reshape(groups_n * capacity, width)[slot]
    loss2_rows = back_loss.reshape(groups_n * capacity)[slot]
    embed_grad = (dx1 + dx2_rows.astype(jnp.float32)).astype(jnp.bfloat16)
    row_loss = loss1 + loss2_rows.astype(jnp.float32)
    return (row_loss, embed_grad, level1_grad, level2_grad)


def nn(a, b):
    return lax.dot_general(a, b, (((1,), (0,)), ((), ())), preferred_element_type=F32)


def nt(a, b):
    return lax.dot_general(a, b, (((1,), (1,)), ((), ())), preferred_element_type=F32)


def tn(a, b):
    return lax.dot_general(a, b, (((0,), (0,)), ((), ())), preferred_element_type=F32)


def upright(row):
    return jnp.transpose(jnp.broadcast_to(row, (LANES, row.shape[1])))[:, 0:1]


def near_kernel(
    me_ref, group_ref, label_ref, weight_ref, rows_ref, theirs_ref, mine_ref, key_ref, aux_ref
):
    cap, _ = mine_ref.shape
    rows_n, _ = rows_ref.shape
    groups_n = 2 * rows_n // cap
    groups = group_ref[...]
    kinds = lax.broadcasted_iota(jnp.int32, (groups_n, rows_n), 0)
    hot = jnp.where(groups == kinds, 1.0, 0.0)
    earlier = lax.broadcasted_iota(jnp.int32, (rows_n, rows_n), 0) < lax.broadcasted_iota(
        jnp.int32, (rows_n, rows_n), 1
    )
    before = nn(hot.astype(BF16), jnp.where(earlier, 1.0, 0.0).astype(BF16))
    rank = jnp.sum(before * hot, axis=0, keepdims=True).astype(jnp.int32)
    key_ref[...] = (groups ^ me_ref[0]) * cap + rank
    kind = lax.broadcasted_iota(jnp.int32, (LANES, rows_n), 0)
    label = label_ref[...]
    weight = weight_ref[...].astype(F32)
    high = (label >> 5).astype(F32)
    low = (label & 31).astype(F32)
    aux_ref[...] = jnp.where(
        kind == 0, weight, jnp.where(kind == 1, high, jnp.where(kind == 2, low, 0.0))
    ).astype(BF16)
    place_rows(key_ref, aux_ref, rows_ref, mine_ref, 2)
    place_rows(key_ref, aux_ref, rows_ref, theirs_ref, 3)


def place_rows(key_ref, aux_ref, rows_ref, out_ref, t):
    cap = out_ref.shape[0]
    rows_n, width = rows_ref.shape
    place = lax.broadcasted_iota(jnp.int32, (cap, rows_n), 0)
    pick = jnp.where(key_ref[...] == place + t * cap, 1.0, 0.0).astype(BF16)
    out_ref[:, :width] = nn(pick, rows_ref[...]).astype(BF16)
    out_ref[:, width:] = nt(pick, aux_ref[...]).astype(BF16)


def near_rows(me, groups, labels, weights, rows, cap):
    rows_n, width = rows.shape
    full = width + LANES
    vmem = pl.BlockSpec(memory_space=pltpu.VMEM)
    out = jax.ShapeDtypeStruct((cap, full), BF16)
    return pl.pallas_call(
        near_kernel,
        in_specs=[pl.BlockSpec(memory_space=pltpu.SMEM)] + [vmem] * 4,
        out_specs=[vmem] * 4,
        out_shape=[
            out,
            out,
            jax.ShapeDtypeStruct((1, rows_n), jnp.int32),
            jax.ShapeDtypeStruct((LANES, rows_n), BF16),
        ],
        cost_estimate=pl.CostEstimate(
            flops=6 * cap * rows_n * full,
            bytes_accessed=2 * (rows_n * width + 2 * cap * full),
            transcendentals=0,
        ),
        name="near_rows",
    )(me, groups, labels, weights, rows)


def prepare_kernel(
    key_ref, aux_ref, group_ref, weight_ref, w1_ref, rows_ref,
    theirs_ref, mine_ref, loss_ref, dz_ref, grad_ref,
):
    s = pl.program_id(0)
    slot = jnp.where(s == 0, 0, s + 1)
    groups_n = w1_ref.shape[0]
    rows_n = rows_ref.shape[0]
    place_rows(key_ref, aux_ref, rows_ref, theirs_ref, 2 * slot + 1)
    place_rows(key_ref, aux_ref, rows_ref, mine_ref, 2 * slot)

    @pl.when(s == 0)
    def _():
        kinds = lax.broadcasted_iota(jnp.int32, (groups_n, rows_n), 0)
        hot = jnp.where(group_ref[...] == kinds, 1.0, 0.0)
        weight = weight_ref[...].astype(F32)
        z = nt(w1_ref[...], rows_ref[...])
        top = jnp.max(z, axis=0, keepdims=True)
        exps = jnp.exp(z - top)
        mass = jnp.sum(exps, axis=0, keepdims=True)
        loss_ref[...] = top + jnp.log(mass) - jnp.sum(z * hot, axis=0, keepdims=True)
        dz = (weight * (exps / mass - hot)).astype(BF16)
        dz_ref[...] = dz
        grad_ref[...] = nn(dz, rows_ref[...])


def prepare(key, aux, groups, weights, w1, rows, cap):
    rows_n, width = rows.shape
    groups_n = w1.shape[0]
    full = width + LANES
    slots = groups_n // 2 - 1
    out = jax.ShapeDtypeStruct((slots, cap, full), BF16)
    block = pl.BlockSpec((pl.Squeezed(), cap, full), lambda s: (s, 0, 0))
    flat = lambda *shape: pl.BlockSpec(shape, lambda s: (0, 0))
    line = flat(1, rows_n)
    return pl.pallas_call(
        prepare_kernel,
        grid=(slots,),
        in_specs=[
            line, flat(LANES, rows_n), line, line, flat(groups_n, width), flat(rows_n, width),
        ],
        out_specs=[block, block, line, flat(groups_n, rows_n), flat(groups_n, width)],
        out_shape=[
            out,
            out,
            jax.ShapeDtypeStruct((1, rows_n), F32),
            jax.ShapeDtypeStruct((groups_n, rows_n), BF16),
            jax.ShapeDtypeStruct((groups_n, width), F32),
        ],
        cost_estimate=pl.CostEstimate(
            flops=4 * slots * cap * rows_n * full,
            bytes_accessed=2 * (rows_n * width + 2 * slots * cap * full),
            transcendentals=0,
        ),
        name="prepare",
    )(key, aux, groups, weights, w1, rows)


def rows_kernel(picks, n_pieces, n_extra, cap, with_grads, meta_ref, *refs):
    n_blocks = len(picks)
    blocks, refs = refs[:n_blocks], refs[n_blocks:]
    pieces, refs = refs[:n_pieces], refs[n_pieces:]
    extra, refs = refs[:n_extra], refs[n_extra:]
    outs, refs = refs[:n_blocks], refs[n_blocks:]
    if with_grads:
        grad_outs, refs = refs[:4], refs[4:]
        x_s, w_s, dz_s, dx_s, g_s, sems = refs
    else:
        dz_out, refs = refs[0], refs[1:]
        x_s, w_s, dz_s, dx_s, sems = refs
    width, concepts = w_s.shape
    total = n_blocks * cap
    copies = []

    def start(src, dst, n):
        copies.append(pltpu.make_async_copy(src, dst, sems.at[n]))
        copies[-1].start()

    def drain():
        for copy in copies:
            copy.wait()
        copies.clear()

    for i, piece in enumerate(pieces):
        at = pl.multiple_of(meta_ref[i], LANES)
        start(piece, w_s.at[pl.ds(at, piece.shape[0])], i)
    for i, (block, pick) in enumerate(zip(blocks, picks)):
        src = block if pick is None else block.at[pick]
        start(src, x_s.at[pl.ds(i * cap, cap)], n_pieces + i)
    drain()
    for i, block in enumerate(extra[:-1]):
        start(block, x_s.at[pl.ds(total + i * cap, cap)], i)
    if extra:
        start(extra[-1], dz_s.at[pl.ds(total, extra[-1].shape[0])], n_extra)
    later = list(copies)
    copies.clear()
    column = lax.broadcasted_iota(jnp.int32, (cap, concepts), 1)

    @pl.loop(0, n_blocks)
    def _(b):
        here = pl.ds(pl.multiple_of(b * cap, cap), cap)
        z = nn(x_s[here, :width], w_s[...])
        aux = x_s[here, width:].astype(F32)
        weight = aux[:, 0:1]
        label = (aux[:, 1:2] * 32.0 + aux[:, 2:3]).astype(jnp.int32)
        hot = column == label
        top = jnp.max(z, axis=1, keepdims=True)
        exps = jnp.exp(z - top)
        mass = jnp.sum(exps, axis=1, keepdims=True)
        picked = jnp.sum(jnp.where(hot, z, 0.0), axis=1, keepdims=True)
        probs = exps * (1.0 / mass)
        dz = (weight * (probs - jnp.where(hot, 1.0, 0.0))).astype(BF16)
        dz_s[here, :] = dz
        dx_s[here, :width] = nt(dz, w_s[...]).astype(BF16)
        loss = top + jnp.log(mass) - picked
        dx_s[here, width:] = jnp.broadcast_to(loss, (cap, LANES)).astype(BF16)

    for copy in later:
        copy.wait()
    for i, out in enumerate(outs):
        start(dx_s.at[pl.ds(i * cap, cap)], out, i)
    if not with_grads:
        start(dz_s, dz_out, n_blocks)
    else:
        quarter, part = g_s.shape[1], g_s.shape[2]
        for j in range(8):
            at = pl.multiple_of(meta_ref[n_pieces + j], LANES)
            half = (0, 0, 1, 1, 0, 0, 1, 1)[j]
            g_s[j] = tn(
                x_s[:, pl.ds(at, quarter)], dz_s[:, half * part : (half + 1) * part]
            ).astype(BF16)
            if j % 2 == 1:
                start(g_s.at[pl.ds(j - 1, 2)], grad_outs[j // 2], n_blocks + j // 2)
    drain()


def group_step(blocks, pieces, starts, quarters, concepts, cap, extra=(), with_grads=True):
    full = blocks[0][0].shape[-1]
    width = full - LANES
    own_rows = cap * len(blocks)
    total = own_rows + cap * max(len(extra) - 1, 0)
    quarter, part = width // 4, concepts // 2
    meta = jnp.stack(starts + [q * quarter for q in quarters]).astype(jnp.int32)
    hbm = pl.BlockSpec(memory_space=pltpu.HBM)
    dx = jax.ShapeDtypeStruct((cap, full), BF16)
    if with_grads:
        rest = [jax.ShapeDtypeStruct((2, quarter, part), BF16)] * 4
        grad_scratch = [pltpu.VMEM((8, quarter, part), BF16)]
    else:
        rest = [jax.ShapeDtypeStruct((total, concepts), BF16)]
        grad_scratch = []
    n_sems = max(len(pieces) + len(blocks), len(blocks) + 4, len(extra) + 1)
    picks = [i for _, i in blocks]
    res = pl.pallas_call(
        lambda *refs: rows_kernel(picks, len(pieces), len(extra), cap, with_grads, *refs),
        in_specs=[pl.BlockSpec(memory_space=pltpu.SMEM)]
        + [hbm] * (len(blocks) + len(pieces) + len(extra)),
        out_specs=[hbm] * (len(blocks) + len(rest)),
        out_shape=[dx] * len(blocks) + rest,
        scratch_shapes=[
            pltpu.VMEM((total, full), BF16),
            pltpu.VMEM((width, concepts), BF16),
            pltpu.VMEM((total, concepts), BF16),
            pltpu.VMEM((own_rows, full), BF16),
            *grad_scratch,
            pltpu.SemaphoreType.DMA((n_sems,)),
        ],
        cost_estimate=pl.CostEstimate(
            flops=(4 * own_rows + 2 * total * with_grads) * width * concepts,
            bytes_accessed=4 * (total * full + width * concepts),
            transcendentals=own_rows * concepts,
        ),
    )(meta, *[a for a, _ in blocks], *pieces, *extra)
    return res[: len(blocks)], res[len(blocks) :]


def combine_kernel(n_blocks, cap, key_ref, loss_ref, dz1_ref, w1_ref, *refs):
    blocks, refs = refs[:n_blocks], refs[n_blocks:]
    out_ref, row_loss_ref, x_s, sems = refs

    @pl.when(pl.program_id(0) == 0)
    def _():
        copies = [
            pltpu.make_async_copy(b, x_s.at[pl.ds(i * cap, cap)], sems.at[i])
            for i, b in enumerate(blocks)
        ]
        for copy in copies:
            copy.start()
        for copy in copies:
            copy.wait()

    tile, width = out_ref.shape
    slots = x_s.shape[0]
    place = lax.broadcasted_iota(jnp.int32, (tile, slots), 1)
    pick = jnp.where(upright(key_ref[...]) == place, 1.0, 0.0).astype(BF16)
    got = nn(pick, x_s[...])
    dx1 = tn(dz1_ref[...], w1_ref[...])
    out_ref[...] = (dx1 + got[:, :width]).astype(BF16)
    row_loss_ref[...] = loss_ref[...] + jnp.transpose(got[:, width:])[0:1, :]


def combine(key, loss1, dz1, w1, blocks, cap):
    rows_n = key.shape[1]
    groups_n, width = w1.shape
    full = width + LANES
    tile = cap
    slots = cap * len(blocks)
    line = pl.BlockSpec((1, tile), lambda i: (0, i))
    return pl.pallas_call(
        lambda *refs: combine_kernel(len(blocks), cap, *refs),
        grid=(rows_n // tile,),
        in_specs=[
            line,
            line,
            pl.BlockSpec((groups_n, tile), lambda i: (0, i)),
            pl.BlockSpec((groups_n, width), lambda i: (0, 0)),
        ]
        + [pl.BlockSpec(memory_space=pltpu.HBM)] * len(blocks),
        out_specs=[pl.BlockSpec((tile, width), lambda i: (i, 0)), line],
        out_shape=[
            jax.ShapeDtypeStruct((rows_n, width), BF16),
            jax.ShapeDtypeStruct((1, rows_n), F32),
        ],
        scratch_shapes=[
            pltpu.VMEM((slots, full), BF16),
            pltpu.SemaphoreType.DMA((len(blocks),)),
        ],
        cost_estimate=pl.CostEstimate(
            flops=2 * rows_n * slots * full,
            bytes_accessed=2 * (slots * full + rows_n * width),
            transcendentals=0,
        ),
        name="combine",
    )(key, loss1, dz1, w1, *blocks)


def make_local(dp_n, concept_n):
    def pairs(dp_bit, concept_bit):
        return [
            (d * concept_n + c, (d ^ dp_bit) * concept_n + (c ^ concept_bit))
            for d in range(dp_n)
            for c in range(concept_n)
        ]

    core, near, cross, far, away, side, up = (
        pairs(0, 1),
        pairs(0, 2),
        pairs(0, 3),
        pairs(0, 4),
        pairs(0, 6),
        pairs(1, 0),
        pairs(2, 0),
    )

    def send(a, to):
        return lax.ppermute(a, AXES, to)

    def local(embeddings, row_weight, group_label, concept_label, level1_weight, level2_weight):
        return body(
            embeddings, row_weight, group_label, concept_label, level1_weight, level2_weight
        )

    def body(embeddings, row_weight, group_label, concept_label, level1_weight, level2_weight):
        rows_n, width = embeddings.shape
        groups_n = level1_weight.shape[1]
        concepts = level2_weight.shape[2]
        cap = 2 * rows_n // groups_n
        quarter = width // dp_n
        piece = quarter // PIECES
        dp, me = lax.axis_index("dp"), lax.axis_index("concept")

        own = level2_weight[0]

        def spread(q, h):
            qx, qy = send(q, side), send(q, up)
            last = send(qx, up) if h % 2 == 0 else send(qy, side)
            return [q, qx, qy, last]

        pieces2, pieces3, starts = [], [], []
        for h in range(PIECES):
            first = lax.dynamic_slice_in_dim(own, dp * quarter + h * piece, piece, 0)
            far2 = send(first, far)
            far3 = send(far2, near)
            pieces2 += spread(far2, h)
            pieces3 += spread(far3, h)
            starts += [(dp ^ i) * quarter + h * piece for i in range(4)]
        order = [dp ^ 1, dp ^ 3, dp ^ 2, dp ^ 3, dp, dp ^ 2, dp, dp ^ 1]

        w1 = level1_weight.T
        groups, weights = group_label.T, row_weight[None, :]
        theirs1, mine1, key, aux = near_rows(
            me[None].astype(jnp.int32),
            groups,
            concept_label[None, :],
            weights,
            embeddings,
            cap,
        )
        rows_in = [send(mine1, near), send(theirs1, cross)]
        theirs, mine, loss1, dz1, grad1 = prepare(key, aux, groups, weights, w1, embeddings, cap)
        got = send(theirs, core)
        for to in (core, side, up, near, far):
            grad1 = grad1 + send(grad1, to)

        whole = [jnp.zeros((), jnp.int32)]

        def step(blocks, pieces, at, **kw):
            return group_step(blocks, pieces, at, order, concepts, cap, **kw)

        dx_1, (dz_in,) = step([(r, None) for r in rows_in], [own], whole, with_grads=False)
        dx_2, grads_2 = step([(mine, 1), (got, 1)], pieces2, starts)
        dx_3, grads_3 = step([(mine, 2), (got, 2)], pieces3, starts)
        dx_0, grads_0 = step([(mine, 0), (got, 0)], [own], whole, extra=(*rows_in, dz_in))

        def scatter(grads):
            to_x, to_y, keep_a, keep_b = (g for g in grads)
            from_x, from_y = send(to_x, side), send(to_y, up)
            pass_a = (keep_a[1].astype(F32) + from_x[1].astype(F32)).astype(BF16)
            pass_b = (keep_b[1].astype(F32) + from_y[1].astype(F32)).astype(BF16)
            last_a = send(pass_a, up)
            last_b = send(pass_b, side)
            sum_a = keep_a[0].astype(F32) + from_x[0].astype(F32) + last_a.astype(F32)
            sum_b = keep_b[0].astype(F32) + from_y[0].astype(F32) + last_b.astype(F32)
            return sum_a, sum_b

        def join(a, b):
            return jnp.concatenate([a, b], axis=1)

        sum2 = join(*scatter(grads_2)).astype(BF16)
        sum3 = join(*scatter(grads_3)).astype(BF16)
        parts0 = scatter(grads_0)
        from2, from3 = send(sum2, far), send(sum3, away)
        level2_grad = (join(*parts0) + from2.astype(F32) + from3.astype(F32)).astype(BF16)

        home = [
            dx_0[0],
            send(dx_0[1], core),
            send(dx_1[0], near),
            send(dx_1[1], cross),
            dx_2[0],
            send(dx_2[1], core),
            dx_3[0],
            send(dx_3[1], core),
        ]
        embed_grad, row_loss = combine(key, loss1, dz1, w1, home, cap)
        return (row_loss[0], embed_grad, grad1.T, level2_grad[None])

    return local


def solution(mesh):
    dp_n, concept_n = mesh.shape["dp"], mesh.shape["concept"]
    few = dp_n == 4 and concept_n == 8
    return jax.shard_map(
        make_local(dp_n, concept_n) if few else on_device,
        mesh=mesh,
        in_specs=(
            P(("dp", "concept"), None),
            P(("dp", "concept")),
            P(("dp", "concept"), None),
            P(("dp", "concept")),
            P(),
            P("concept", None, None),
        ),
        out_specs=(P(("dp", "concept")), P(("dp", "concept"), None), P(), P("concept", "dp", None)),
        check_vma=False,
    )
```

```python
import jax
import jax.numpy as jnp
from jax import lax
from jax.experimental import pallas as pl
from jax.experimental.pallas import tpu as pltpu
from jax.sharding import PartitionSpec as P

LANES = 128
PIECES = 2
F32, BF16 = jnp.float32, jnp.bfloat16
AXES = ("dp", "concept")


def first_level(embeddings, weights, groups, level1_weight):
    groups_n = level1_weight.shape[1]
    z1 = jnp.dot(embeddings, level1_weight, preferred_element_type=jnp.float32)
    top1 = jnp.max(z1, axis=1, keepdims=True)
    exps1 = jnp.exp(z1 - top1)
    total1 = jnp.sum(exps1, axis=1, keepdims=True)
    probs1 = exps1 / total1
    onehot1 = (groups[:, None] == jnp.arange(groups_n, dtype=jnp.int32)[None, :]).astype(
        jnp.float32
    )
    loss1 = top1[:, 0] + jnp.log(total1[:, 0]) - jnp.sum(z1 * onehot1, axis=1)
    dz1 = (weights[:, None] * (probs1 - onehot1)).astype(jnp.bfloat16)
    partial_grad = lax.dot_general(
        embeddings, dz1, (((0,), (0,)), ((), ())), preferred_element_type=jnp.float32
    )
    dx1 = jnp.dot(dz1, level1_weight.T, preferred_element_type=jnp.float32)
    level1_grad = lax.psum(partial_grad, ("dp", "concept"))
    return (loss1, dx1, level1_grad)


def on_device(embeddings, row_weight, group_label, concept_label, level1_weight, level2_weight):
    rows_n, width = embeddings.shape
    groups_n = level1_weight.shape[1]
    concepts = level2_weight.shape[2]
    capacity = 2 * rows_n // groups_n
    groups = group_label[:, 0]
    weights = row_weight.astype(jnp.float32)
    member = (groups[:, None] == jnp.arange(groups_n, dtype=jnp.int32)[None, :]).astype(
        jnp.bfloat16
    )
    positions = jnp.arange(rows_n, dtype=jnp.int32)
    earlier = (positions[None, :] < positions[:, None]).astype(jnp.bfloat16)
    before = jnp.dot(earlier, member, preferred_element_type=jnp.float32)
    rank = jnp.sum(before * member.astype(jnp.float32), axis=1).astype(jnp.int32)
    slot = groups * capacity + rank
    source = jnp.full((groups_n * capacity,), rows_n, jnp.int32).at[slot].set(positions)
    filled = source < rows_n
    safe = jnp.minimum(source, rows_n - 1)
    send_rows = jnp.where(filled[:, None], embeddings[safe], jnp.zeros((), jnp.bfloat16)).reshape(
        groups_n, capacity, width
    )
    send_weight = jnp.where(filled, row_weight[safe], jnp.zeros((), jnp.bfloat16)).reshape(
        groups_n, capacity
    )
    send_label = jnp.where(filled, concept_label[safe], 0).reshape(groups_n, capacity)
    loss1, dx1, level1_grad = first_level(embeddings, weights, groups, level1_weight)
    recv_rows, recv_weight, recv_label = (
        lax.all_to_all(send_rows, "concept", split_axis=0, concat_axis=1, tiled=True),
        lax.all_to_all(send_weight, "concept", split_axis=0, concat_axis=1, tiled=True),
        lax.all_to_all(send_label, "concept", split_axis=0, concat_axis=1, tiled=True),
    )
    z2 = jnp.einsum("grd,gdc->grc", recv_rows, level2_weight, preferred_element_type=jnp.float32)
    top2 = jnp.max(z2, axis=2, keepdims=True)
    exps2 = jnp.exp(z2 - top2)
    total2 = jnp.sum(exps2, axis=2, keepdims=True)
    probs2 = exps2 / total2
    onehot2 = (
        recv_label[:, :, None] == jnp.arange(concepts, dtype=jnp.int32)[None, None, :]
    ).astype(jnp.float32)
    loss2 = (top2[:, :, 0] + jnp.log(total2[:, :, 0]) - jnp.sum(z2 * onehot2, axis=2)).astype(
        jnp.bfloat16
    )
    dz2 = (recv_weight.astype(jnp.float32)[:, :, None] * (probs2 - onehot2)).astype(jnp.bfloat16)
    dx2 = jnp.einsum("grc,gdc->grd", dz2, level2_weight, preferred_element_type=jnp.float32).astype(
        jnp.bfloat16
    )
    back_grad, back_loss = (
        lax.all_to_all(dx2, "concept", split_axis=1, concat_axis=0, tiled=True),
        lax.all_to_all(loss2, "concept", split_axis=1, concat_axis=0, tiled=True),
    )
    summed = lax.psum_scatter(
        jnp.einsum("grd,grc->dgc", recv_rows, dz2, preferred_element_type=jnp.float32),
        "dp",
        scatter_dimension=0,
        tiled=True,
    )
    level2_grad = jnp.transpose(summed, (1, 0, 2)).astype(jnp.bfloat16)
    dx2_rows = back_grad.reshape(groups_n * capacity, width)[slot]
    loss2_rows = back_loss.reshape(groups_n * capacity)[slot]
    embed_grad = (dx1 + dx2_rows.astype(jnp.float32)).astype(jnp.bfloat16)
    row_loss = loss1 + loss2_rows.astype(jnp.float32)
    return (row_loss, embed_grad, level1_grad, level2_grad)


def nn(a, b):
    return lax.dot_general(a, b, (((1,), (0,)), ((), ())), preferred_element_type=F32)


def nt(a, b):
    return lax.dot_general(a, b, (((1,), (1,)), ((), ())), preferred_element_type=F32)


def tn(a, b):
    return lax.dot_general(a, b, (((0,), (0,)), ((), ())), preferred_element_type=F32)


def upright(row):
    return jnp.transpose(jnp.broadcast_to(row, (LANES, row.shape[1])))[:, 0:1]


def near_kernel(
    me_ref, group_ref, label_ref, weight_ref, rows_ref, theirs_ref, mine_ref, key_ref, aux_ref
):
    cap, _ = mine_ref.shape
    rows_n, _ = rows_ref.shape
    groups_n = 2 * rows_n // cap
    groups = group_ref[...]
    kinds = lax.broadcasted_iota(jnp.int32, (groups_n, rows_n), 0)
    hot = jnp.where(groups == kinds, 1.0, 0.0)
    earlier = lax.broadcasted_iota(jnp.int32, (rows_n, rows_n), 0) < lax.broadcasted_iota(
        jnp.int32, (rows_n, rows_n), 1
    )
    before = nn(hot.astype(BF16), jnp.where(earlier, 1.0, 0.0).astype(BF16))
    rank = jnp.sum(before * hot, axis=0, keepdims=True).astype(jnp.int32)
    key_ref[...] = (groups ^ me_ref[0]) * cap + rank
    kind = lax.broadcasted_iota(jnp.int32, (LANES, rows_n), 0)
    label = label_ref[...]
    weight = weight_ref[...].astype(F32)
    high = (label >> 5).astype(F32)
    low = (label & 31).astype(F32)
    aux_ref[...] = jnp.where(
        kind == 0, weight, jnp.where(kind == 1, high, jnp.where(kind == 2, low, 0.0))
    ).astype(BF16)
    place_rows(key_ref, aux_ref, rows_ref, mine_ref, 2)
    place_rows(key_ref, aux_ref, rows_ref, theirs_ref, 3)


def place_rows(key_ref, aux_ref, rows_ref, out_ref, t):
    cap = out_ref.shape[0]
    rows_n, width = rows_ref.shape
    place = lax.broadcasted_iota(jnp.int32, (cap, rows_n), 0)
    pick = jnp.where(key_ref[...] == place + t * cap, 1.0, 0.0).astype(BF16)
    out_ref[:, :width] = nn(pick, rows_ref[...]).astype(BF16)
    out_ref[:, width:] = nt(pick, aux_ref[...]).astype(BF16)


def near_rows(me, groups, labels, weights, rows, cap):
    rows_n, width = rows.shape
    full = width + LANES
    vmem = pl.BlockSpec(memory_space=pltpu.VMEM)
    out = jax.ShapeDtypeStruct((cap, full), BF16)
    return pl.pallas_call(
        near_kernel,
        in_specs=[pl.BlockSpec(memory_space=pltpu.SMEM)] + [vmem] * 4,
        out_specs=[vmem] * 4,
        out_shape=[
            out,
            out,
            jax.ShapeDtypeStruct((1, rows_n), jnp.int32),
            jax.ShapeDtypeStruct((LANES, rows_n), BF16),
        ],
        cost_estimate=pl.CostEstimate(
            flops=6 * cap * rows_n * full,
            bytes_accessed=2 * (rows_n * width + 2 * cap * full),
            transcendentals=0,
        ),
        name="near_rows",
    )(me, groups, labels, weights, rows)


def prepare_kernel(
    key_ref, aux_ref, group_ref, weight_ref, w1_ref, rows_ref,
    theirs_ref, mine_ref, loss_ref, dz_ref, grad_ref,
):
    s = pl.program_id(0)
    slot = jnp.where(s == 0, 0, s + 1)
    groups_n = w1_ref.shape[0]
    rows_n = rows_ref.shape[0]
    place_rows(key_ref, aux_ref, rows_ref, theirs_ref, 2 * slot + 1)
    place_rows(key_ref, aux_ref, rows_ref, mine_ref, 2 * slot)

    @pl.when(s == 0)
    def _():
        kinds = lax.broadcasted_iota(jnp.int32, (groups_n, rows_n), 0)
        hot = jnp.where(group_ref[...] == kinds, 1.0, 0.0)
        weight = weight_ref[...].astype(F32)
        z = nt(w1_ref[...], rows_ref[...])
        top = jnp.max(z, axis=0, keepdims=True)
        exps = jnp.exp(z - top)
        mass = jnp.sum(exps, axis=0, keepdims=True)
        loss_ref[...] = top + jnp.log(mass) - jnp.sum(z * hot, axis=0, keepdims=True)
        dz = (weight * (exps / mass - hot)).astype(BF16)
        dz_ref[...] = dz
        grad_ref[...] = nn(dz, rows_ref[...])


def prepare(key, aux, groups, weights, w1, rows, cap):
    rows_n, width = rows.shape
    groups_n = w1.shape[0]
    full = width + LANES
    slots = groups_n // 2 - 1
    out = jax.ShapeDtypeStruct((slots, cap, full), BF16)
    block = pl.BlockSpec((pl.Squeezed(), cap, full), lambda s: (s, 0, 0))
    flat = lambda *shape: pl.BlockSpec(shape, lambda s: (0, 0))
    line = flat(1, rows_n)
    return pl.pallas_call(
        prepare_kernel,
        grid=(slots,),
        in_specs=[
            line, flat(LANES, rows_n), line, line, flat(groups_n, width), flat(rows_n, width),
        ],
        out_specs=[block, block, line, flat(groups_n, rows_n), flat(groups_n, width)],
        out_shape=[
            out,
            out,
            jax.ShapeDtypeStruct((1, rows_n), F32),
            jax.ShapeDtypeStruct((groups_n, rows_n), BF16),
            jax.ShapeDtypeStruct((groups_n, width), F32),
        ],
        cost_estimate=pl.CostEstimate(
            flops=4 * slots * cap * rows_n * full,
            bytes_accessed=2 * (rows_n * width + 2 * slots * cap * full),
            transcendentals=0,
        ),
        name="prepare",
    )(key, aux, groups, weights, w1, rows)


def rows_kernel(picks, starts, n_extra, cap, with_grads, meta_ref, *refs):
    n_blocks, n_pieces = len(picks), len(starts)
    blocks, refs = refs[:n_blocks], refs[n_blocks:]
    pieces, refs = refs[:n_pieces], refs[n_pieces:]
    extra, refs = refs[:n_extra], refs[n_extra:]
    outs, refs = refs[:n_blocks], refs[n_blocks:]
    if with_grads:
        grad_outs, refs = refs[:4], refs[4:]
        x_s, w_s, dz_s, dx_s, g_s, sems = refs
    else:
        dz_out, refs = refs[0], refs[1:]
        x_s, w_s, dz_s, dx_s, sems = refs
    width, concepts = w_s.shape
    total = n_blocks * cap
    copies = []

    def start(src, dst, n):
        copies.append(pltpu.make_async_copy(src, dst, sems.at[n]))
        copies[-1].start()

    def drain():
        for copy in copies:
            copy.wait()
        copies.clear()

    for i, piece in enumerate(pieces):
        at = 0
        if starts[i] is not None:
            flip, shift = starts[i]
            at = pl.multiple_of((meta_ref[0] ^ flip) * (width // 4) + shift, LANES)
        start(piece, w_s.at[pl.ds(at, piece.shape[0])], i)
    for i, (block, pick) in enumerate(zip(blocks, picks)):
        src = block if pick is None else block.at[pick]
        start(src, x_s.at[pl.ds(i * cap, cap)], n_pieces + i)
    drain()
    for i, block in enumerate(extra[:-1]):
        start(block, x_s.at[pl.ds(total + i * cap, cap)], i)
    if extra:
        start(extra[-1], dz_s.at[pl.ds(total, extra[-1].shape[0])], n_extra)
    later = list(copies)
    copies.clear()
    column = lax.broadcasted_iota(jnp.int32, (cap, concepts), 1)

    @pl.loop(0, n_blocks)
    def _(b):
        here = pl.ds(pl.multiple_of(b * cap, cap), cap)
        z = nn(x_s[here, :width], w_s[...])
        aux = x_s[here, width:].astype(F32)
        weight = aux[:, 0:1]
        label = (aux[:, 1:2] * 32.0 + aux[:, 2:3]).astype(jnp.int32)
        hot = column == label
        top = jnp.max(z, axis=1, keepdims=True)
        exps = jnp.exp(z - top)
        mass = jnp.sum(exps, axis=1, keepdims=True)
        picked = jnp.sum(jnp.where(hot, z, 0.0), axis=1, keepdims=True)
        probs = exps * (1.0 / mass)
        dz = (weight * (probs - jnp.where(hot, 1.0, 0.0))).astype(BF16)
        dz_s[here, :] = dz
        dx_s[here, :width] = nt(dz, w_s[...]).astype(BF16)
        loss = top + jnp.log(mass) - picked
        dx_s[here, width:] = jnp.broadcast_to(loss, (cap, LANES)).astype(BF16)

    for copy in later:
        copy.wait()
    for i, out in enumerate(outs):
        start(dx_s.at[pl.ds(i * cap, cap)], out, i)
    if not with_grads:
        start(dz_s, dz_out, n_blocks)
    else:
        quarter, part = g_s.shape[1], g_s.shape[2]
        for j in range(8):
            at = pl.multiple_of((meta_ref[0] ^ (1, 3, 2, 3, 0, 2, 0, 1)[j]) * quarter, LANES)
            half = (0, 0, 1, 1, 0, 0, 1, 1)[j]
            g_s[j] = tn(
                x_s[:, pl.ds(at, quarter)], dz_s[:, half * part : (half + 1) * part]
            ).astype(BF16)
            if j % 2 == 1:
                start(g_s.at[pl.ds(j - 1, 2)], grad_outs[j // 2], n_blocks + j // 2)
    drain()


def group_step(blocks, pieces, starts, meta, concepts, cap, extra=(), with_grads=True):
    full = blocks[0][0].shape[-1]
    width = full - LANES
    own_rows = cap * len(blocks)
    total = own_rows + cap * max(len(extra) - 1, 0)
    quarter, part = width // 4, concepts // 2
    hbm = pl.BlockSpec(memory_space=pltpu.HBM)
    dx = jax.ShapeDtypeStruct((cap, full), BF16)
    if with_grads:
        rest = [jax.ShapeDtypeStruct((2, quarter, part), BF16)] * 4
        grad_scratch = [pltpu.VMEM((8, quarter, part), BF16)]
    else:
        rest = [jax.ShapeDtypeStruct((total, concepts), BF16)]
        grad_scratch = []
    n_sems = max(len(pieces) + len(blocks), len(blocks) + 4, len(extra) + 1)
    picks = [i for _, i in blocks]
    res = pl.pallas_call(
        lambda *refs: rows_kernel(picks, starts, len(extra), cap, with_grads, *refs),
        in_specs=[pl.BlockSpec(memory_space=pltpu.SMEM)]
        + [hbm] * (len(blocks) + len(pieces) + len(extra)),
        out_specs=[hbm] * (len(blocks) + len(rest)),
        out_shape=[dx] * len(blocks) + rest,
        scratch_shapes=[
            pltpu.VMEM((total, full), BF16),
            pltpu.VMEM((width, concepts), BF16),
            pltpu.VMEM((total, concepts), BF16),
            pltpu.VMEM((own_rows, full), BF16),
            *grad_scratch,
            pltpu.SemaphoreType.DMA((n_sems,)),
        ],
        cost_estimate=pl.CostEstimate(
            flops=(4 * own_rows + 2 * total * with_grads) * width * concepts,
            bytes_accessed=4 * (total * full + width * concepts),
            transcendentals=own_rows * concepts,
        ),
    )(meta, *[a for a, _ in blocks], *pieces, *extra)
    return res[: len(blocks)], res[len(blocks) :]


def combine_kernel(n_blocks, cap, key_ref, loss_ref, dz1_ref, w1_ref, *refs):
    blocks, refs = refs[:n_blocks], refs[n_blocks:]
    out_ref, row_loss_ref, x_s, sems = refs

    @pl.when(pl.program_id(0) == 0)
    def _():
        copies = [
            pltpu.make_async_copy(b, x_s.at[pl.ds(i * cap, cap)], sems.at[i])
            for i, b in enumerate(blocks)
        ]
        for copy in copies:
            copy.start()
        for copy in copies:
            copy.wait()

    tile, width = out_ref.shape
    slots = x_s.shape[0]
    place = lax.broadcasted_iota(jnp.int32, (tile, slots), 1)
    pick = jnp.where(upright(key_ref[...]) == place, 1.0, 0.0).astype(BF16)
    got = nn(pick, x_s[...])
    dx1 = tn(dz1_ref[...], w1_ref[...])
    out_ref[...] = (dx1 + got[:, :width]).astype(BF16)
    row_loss_ref[...] = loss_ref[...] + jnp.transpose(got[:, width:])[0:1, :]


def combine(key, loss1, dz1, w1, blocks, cap):
    rows_n = key.shape[1]
    groups_n, width = w1.shape
    full = width + LANES
    tile = cap
    slots = cap * len(blocks)
    line = pl.BlockSpec((1, tile), lambda i: (0, i))
    return pl.pallas_call(
        lambda *refs: combine_kernel(len(blocks), cap, *refs),
        grid=(rows_n // tile,),
        in_specs=[
            line,
            line,
            pl.BlockSpec((groups_n, tile), lambda i: (0, i)),
            pl.BlockSpec((groups_n, width), lambda i: (0, 0)),
        ]
        + [pl.BlockSpec(memory_space=pltpu.HBM)] * len(blocks),
        out_specs=[pl.BlockSpec((tile, width), lambda i: (i, 0)), line],
        out_shape=[
            jax.ShapeDtypeStruct((rows_n, width), BF16),
            jax.ShapeDtypeStruct((1, rows_n), F32),
        ],
        scratch_shapes=[
            pltpu.VMEM((slots, full), BF16),
            pltpu.SemaphoreType.DMA((len(blocks),)),
        ],
        cost_estimate=pl.CostEstimate(
            flops=2 * rows_n * slots * full,
            bytes_accessed=2 * (slots * full + rows_n * width),
            transcendentals=0,
        ),
        name="combine",
    )(key, loss1, dz1, w1, *blocks)


def make_local(dp_n, concept_n):
    def pairs(dp_bit, concept_bit):
        return [
            (d * concept_n + c, (d ^ dp_bit) * concept_n + (c ^ concept_bit))
            for d in range(dp_n)
            for c in range(concept_n)
        ]

    core, near, cross, far, away, side, up = (
        pairs(0, 1),
        pairs(0, 2),
        pairs(0, 3),
        pairs(0, 4),
        pairs(0, 6),
        pairs(1, 0),
        pairs(2, 0),
    )

    def send(a, to):
        return lax.ppermute(a, AXES, to)

    def local(embeddings, row_weight, group_label, concept_label, level1_weight, level2_weight):
        return body(
            embeddings, row_weight, group_label, concept_label, level1_weight, level2_weight
        )

    def body(embeddings, row_weight, group_label, concept_label, level1_weight, level2_weight):
        rows_n, width = embeddings.shape
        groups_n = level1_weight.shape[1]
        concepts = level2_weight.shape[2]
        cap = 2 * rows_n // groups_n
        quarter = width // dp_n
        piece = quarter // PIECES
        dp, me = lax.axis_index("dp"), lax.axis_index("concept")

        own = level2_weight[0]

        def spread(q, h):
            qx, qy = send(q, side), send(q, up)
            last = send(qx, up) if h % 2 == 0 else send(qy, side)
            return [q, qx, qy, last]

        pieces2, pieces3, starts = [], [], []
        for h in range(PIECES):
            first = lax.dynamic_slice_in_dim(own, dp * quarter + h * piece, piece, 0)
            far2 = send(first, far)
            far3 = send(far2, near)
            pieces2 += spread(far2, h)
            pieces3 += spread(far3, h)
            starts += [(i, h * piece) for i in range(4)]
        here = dp[None].astype(jnp.int32)

        w1 = level1_weight.T
        groups, weights = group_label.T, row_weight[None, :]
        theirs1, mine1, key, aux = near_rows(
            me[None].astype(jnp.int32),
            groups,
            concept_label[None, :],
            weights,
            embeddings,
            cap,
        )
        rows_in = [send(mine1, near), send(theirs1, cross)]
        theirs, mine, loss1, dz1, grad1 = prepare(key, aux, groups, weights, w1, embeddings, cap)
        got = send(theirs, core)
        for to in (core, side, up, near, far):
            grad1 = grad1 + send(grad1, to)

        whole = [None]

        def step(blocks, pieces, at, **kw):
            return group_step(blocks, pieces, at, here, concepts, cap, **kw)

        dx_1, (dz_in,) = step([(r, None) for r in rows_in], [own], whole, with_grads=False)
        dx_2, grads_2 = step([(mine, 1), (got, 1)], pieces2, starts)
        dx_3, grads_3 = step([(mine, 2), (got, 2)], pieces3, starts)
        dx_0, grads_0 = step([(mine, 0), (got, 0)], [own], whole, extra=(*rows_in, dz_in))

        def scatter(grads):
            to_x, to_y, keep_a, keep_b = (g for g in grads)
            from_x, from_y = send(to_x, side), send(to_y, up)
            pass_a = (keep_a[1].astype(F32) + from_x[1].astype(F32)).astype(BF16)
            pass_b = (keep_b[1].astype(F32) + from_y[1].astype(F32)).astype(BF16)
            last_a = send(pass_a, up)
            last_b = send(pass_b, side)
            sum_a = keep_a[0].astype(F32) + from_x[0].astype(F32) + last_a.astype(F32)
            sum_b = keep_b[0].astype(F32) + from_y[0].astype(F32) + last_b.astype(F32)
            return sum_a, sum_b

        def join(a, b):
            return jnp.concatenate([a, b], axis=1)

        sum2 = join(*scatter(grads_2)).astype(BF16)
        sum3 = join(*scatter(grads_3)).astype(BF16)
        parts0 = scatter(grads_0)
        from2, from3 = send(sum2, far), send(sum3, away)
        level2_grad = (join(*parts0) + from2.astype(F32) + from3.astype(F32)).astype(BF16)[None]

        home = [
            dx_0[0],
            send(dx_0[1], core),
            send(dx_1[0], near),
            send(dx_1[1], cross),
            dx_2[0],
            send(dx_2[1], core),
            dx_3[0],
            send(dx_3[1], core),
        ]
        embed_grad, row_loss = combine(key, loss1, dz1, w1, home, cap)
        return (row_loss[0], embed_grad, grad1.T, level2_grad)

    return local


def solution(mesh):
    dp_n, concept_n = mesh.shape["dp"], mesh.shape["concept"]
    few = dp_n == 4 and concept_n == 8
    return jax.shard_map(
        make_local(dp_n, concept_n) if few else on_device,
        mesh=mesh,
        in_specs=(
            P(("dp", "concept"), None),
            P(("dp", "concept")),
            P(("dp", "concept"), None),
            P(("dp", "concept")),
            P(),
            P("concept", None, None),
        ),
        out_specs=(P(("dp", "concept")), P(("dp", "concept"), None), P(), P("concept", "dp", None)),
        check_vma=False,
    )
```

```python
import jax
import jax.numpy as jnp
from jax import lax
from jax.experimental import pallas as pl
from jax.experimental.pallas import tpu as pltpu
from jax.sharding import PartitionSpec as P

LANES = 128
PIECES = 2
F32, BF16 = jnp.float32, jnp.bfloat16
AXES = ("dp", "concept")


def first_level(embeddings, weights, groups, level1_weight):
    groups_n = level1_weight.shape[1]
    z1 = jnp.dot(embeddings, level1_weight, preferred_element_type=jnp.float32)
    top1 = jnp.max(z1, axis=1, keepdims=True)
    exps1 = jnp.exp(z1 - top1)
    total1 = jnp.sum(exps1, axis=1, keepdims=True)
    probs1 = exps1 / total1
    onehot1 = (groups[:, None] == jnp.arange(groups_n, dtype=jnp.int32)[None, :]).astype(
        jnp.float32
    )
    loss1 = top1[:, 0] + jnp.log(total1[:, 0]) - jnp.sum(z1 * onehot1, axis=1)
    dz1 = (weights[:, None] * (probs1 - onehot1)).astype(jnp.bfloat16)
    partial_grad = lax.dot_general(
        embeddings, dz1, (((0,), (0,)), ((), ())), preferred_element_type=jnp.float32
    )
    dx1 = jnp.dot(dz1, level1_weight.T, preferred_element_type=jnp.float32)
    level1_grad = lax.psum(partial_grad, ("dp", "concept"))
    return (loss1, dx1, level1_grad)


def on_device(embeddings, row_weight, group_label, concept_label, level1_weight, level2_weight):
    rows_n, width = embeddings.shape
    groups_n = level1_weight.shape[1]
    concepts = level2_weight.shape[2]
    capacity = 2 * rows_n // groups_n
    groups = group_label[:, 0]
    weights = row_weight.astype(jnp.float32)
    member = (groups[:, None] == jnp.arange(groups_n, dtype=jnp.int32)[None, :]).astype(
        jnp.bfloat16
    )
    positions = jnp.arange(rows_n, dtype=jnp.int32)
    earlier = (positions[None, :] < positions[:, None]).astype(jnp.bfloat16)
    before = jnp.dot(earlier, member, preferred_element_type=jnp.float32)
    rank = jnp.sum(before * member.astype(jnp.float32), axis=1).astype(jnp.int32)
    slot = groups * capacity + rank
    source = jnp.full((groups_n * capacity,), rows_n, jnp.int32).at[slot].set(positions)
    filled = source < rows_n
    safe = jnp.minimum(source, rows_n - 1)
    send_rows = jnp.where(filled[:, None], embeddings[safe], jnp.zeros((), jnp.bfloat16)).reshape(
        groups_n, capacity, width
    )
    send_weight = jnp.where(filled, row_weight[safe], jnp.zeros((), jnp.bfloat16)).reshape(
        groups_n, capacity
    )
    send_label = jnp.where(filled, concept_label[safe], 0).reshape(groups_n, capacity)
    loss1, dx1, level1_grad = first_level(embeddings, weights, groups, level1_weight)
    recv_rows, recv_weight, recv_label = (
        lax.all_to_all(send_rows, "concept", split_axis=0, concat_axis=1, tiled=True),
        lax.all_to_all(send_weight, "concept", split_axis=0, concat_axis=1, tiled=True),
        lax.all_to_all(send_label, "concept", split_axis=0, concat_axis=1, tiled=True),
    )
    z2 = jnp.einsum("grd,gdc->grc", recv_rows, level2_weight, preferred_element_type=jnp.float32)
    top2 = jnp.max(z2, axis=2, keepdims=True)
    exps2 = jnp.exp(z2 - top2)
    total2 = jnp.sum(exps2, axis=2, keepdims=True)
    probs2 = exps2 / total2
    onehot2 = (
        recv_label[:, :, None] == jnp.arange(concepts, dtype=jnp.int32)[None, None, :]
    ).astype(jnp.float32)
    loss2 = (top2[:, :, 0] + jnp.log(total2[:, :, 0]) - jnp.sum(z2 * onehot2, axis=2)).astype(
        jnp.bfloat16
    )
    dz2 = (recv_weight.astype(jnp.float32)[:, :, None] * (probs2 - onehot2)).astype(jnp.bfloat16)
    dx2 = jnp.einsum("grc,gdc->grd", dz2, level2_weight, preferred_element_type=jnp.float32).astype(
        jnp.bfloat16
    )
    back_grad, back_loss = (
        lax.all_to_all(dx2, "concept", split_axis=1, concat_axis=0, tiled=True),
        lax.all_to_all(loss2, "concept", split_axis=1, concat_axis=0, tiled=True),
    )
    summed = lax.psum_scatter(
        jnp.einsum("grd,grc->dgc", recv_rows, dz2, preferred_element_type=jnp.float32),
        "dp",
        scatter_dimension=0,
        tiled=True,
    )
    level2_grad = jnp.transpose(summed, (1, 0, 2)).astype(jnp.bfloat16)
    dx2_rows = back_grad.reshape(groups_n * capacity, width)[slot]
    loss2_rows = back_loss.reshape(groups_n * capacity)[slot]
    embed_grad = (dx1 + dx2_rows.astype(jnp.float32)).astype(jnp.bfloat16)
    row_loss = loss1 + loss2_rows.astype(jnp.float32)
    return (row_loss, embed_grad, level1_grad, level2_grad)


def nn(a, b):
    return lax.dot_general(a, b, (((1,), (0,)), ((), ())), preferred_element_type=F32)


def nt(a, b):
    return lax.dot_general(a, b, (((1,), (1,)), ((), ())), preferred_element_type=F32)


def tn(a, b):
    return lax.dot_general(a, b, (((0,), (0,)), ((), ())), preferred_element_type=F32)


def upright(row):
    return jnp.transpose(jnp.broadcast_to(row, (LANES, row.shape[1])))[:, 0:1]


def near_kernel(
    me_ref, group_ref, label_ref, weight_ref, rows_ref, theirs_ref, mine_ref, key_ref, aux_ref
):
    cap, _ = mine_ref.shape
    rows_n, _ = rows_ref.shape
    groups_n = 2 * rows_n // cap
    groups = group_ref[...]
    kinds = lax.broadcasted_iota(jnp.int32, (groups_n, rows_n), 0)
    hot = jnp.where(groups == kinds, 1.0, 0.0)
    earlier = lax.broadcasted_iota(jnp.int32, (rows_n, rows_n), 0) < lax.broadcasted_iota(
        jnp.int32, (rows_n, rows_n), 1
    )
    before = nn(hot.astype(BF16), jnp.where(earlier, 1.0, 0.0).astype(BF16))
    rank = jnp.sum(before * hot, axis=0, keepdims=True).astype(jnp.int32)
    key_ref[...] = (groups ^ me_ref[0]) * cap + rank
    kind = lax.broadcasted_iota(jnp.int32, (LANES, rows_n), 0)
    label = label_ref[...]
    weight = weight_ref[...].astype(F32)
    high = (label >> 5).astype(F32)
    low = (label & 31).astype(F32)
    aux_ref[...] = jnp.where(
        kind == 0, weight, jnp.where(kind == 1, high, jnp.where(kind == 2, low, 0.0))
    ).astype(BF16)
    place_rows(key_ref, aux_ref, rows_ref, mine_ref, 2)
    place_rows(key_ref, aux_ref, rows_ref, theirs_ref, 3)


def place_rows(key_ref, aux_ref, rows_ref, out_ref, t):
    cap = out_ref.shape[0]
    rows_n, width = rows_ref.shape
    place = lax.broadcasted_iota(jnp.int32, (cap, rows_n), 0)
    pick = jnp.where(key_ref[...] == place + t * cap, 1.0, 0.0).astype(BF16)
    out_ref[:, :width] = nn(pick, rows_ref[...]).astype(BF16)
    out_ref[:, width:] = nt(pick, aux_ref[...]).astype(BF16)


def near_rows(me, groups, labels, weights, rows, cap):
    rows_n, width = rows.shape
    full = width + LANES
    vmem = pl.BlockSpec(memory_space=pltpu.VMEM)
    out = jax.ShapeDtypeStruct((cap, full), BF16)
    return pl.pallas_call(
        near_kernel,
        in_specs=[pl.BlockSpec(memory_space=pltpu.SMEM)] + [vmem] * 4,
        out_specs=[vmem] * 4,
        out_shape=[
            out,
            out,
            jax.ShapeDtypeStruct((1, rows_n), jnp.int32),
            jax.ShapeDtypeStruct((LANES, rows_n), BF16),
        ],
        cost_estimate=pl.CostEstimate(
            flops=6 * cap * rows_n * full,
            bytes_accessed=2 * (rows_n * width + 2 * cap * full),
            transcendentals=0,
        ),
        name="near_rows",
    )(me, groups, labels, weights, rows)


def prepare_kernel(
    key_ref, aux_ref, group_ref, weight_ref, w1_ref, rows_ref,
    theirs_ref, mine_ref, loss_ref, dz_ref, grad_ref,
):
    s = pl.program_id(0)
    slot = jnp.where(s == 0, 0, s + 1)
    groups_n = w1_ref.shape[0]
    rows_n = rows_ref.shape[0]
    place_rows(key_ref, aux_ref, rows_ref, theirs_ref, 2 * slot + 1)
    place_rows(key_ref, aux_ref, rows_ref, mine_ref, 2 * slot)

    @pl.when(s == 0)
    def _():
        kinds = lax.broadcasted_iota(jnp.int32, (groups_n, rows_n), 0)
        hot = jnp.where(group_ref[...] == kinds, 1.0, 0.0)
        weight = weight_ref[...].astype(F32)
        z = nt(w1_ref[...], rows_ref[...])
        top = jnp.max(z, axis=0, keepdims=True)
        exps = jnp.exp(z - top)
        mass = jnp.sum(exps, axis=0, keepdims=True)
        loss_ref[...] = top + jnp.log(mass) - jnp.sum(z * hot, axis=0, keepdims=True)
        dz = (weight * (exps / mass - hot)).astype(BF16)
        dz_ref[...] = dz
        grad_ref[...] = nn(dz, rows_ref[...])


def prepare(key, aux, groups, weights, w1, rows, cap):
    rows_n, width = rows.shape
    groups_n = w1.shape[0]
    full = width + LANES
    slots = groups_n // 2 - 1
    out = jax.ShapeDtypeStruct((slots, cap, full), BF16)
    block = pl.BlockSpec((pl.Squeezed(), cap, full), lambda s: (s, 0, 0))
    flat = lambda *shape: pl.BlockSpec(shape, lambda s: (0, 0))
    line = flat(1, rows_n)
    return pl.pallas_call(
        prepare_kernel,
        grid=(slots,),
        in_specs=[
            line, flat(LANES, rows_n), line, line, flat(groups_n, width), flat(rows_n, width),
        ],
        out_specs=[block, block, line, flat(groups_n, rows_n), flat(groups_n, width)],
        out_shape=[
            out,
            out,
            jax.ShapeDtypeStruct((1, rows_n), F32),
            jax.ShapeDtypeStruct((groups_n, rows_n), BF16),
            jax.ShapeDtypeStruct((groups_n, width), F32),
        ],
        cost_estimate=pl.CostEstimate(
            flops=4 * slots * cap * rows_n * full,
            bytes_accessed=2 * (rows_n * width + 2 * slots * cap * full),
            transcendentals=0,
        ),
        name="prepare",
    )(key, aux, groups, weights, w1, rows)


def rows_kernel(picks, starts, n_extra, cap, with_grads, meta_ref, *refs):
    n_blocks, n_pieces = len(picks), len(starts)
    blocks, refs = refs[:n_blocks], refs[n_blocks:]
    pieces, refs = refs[:n_pieces], refs[n_pieces:]
    extra, refs = refs[:n_extra], refs[n_extra:]
    outs, refs = refs[:n_blocks], refs[n_blocks:]
    if with_grads:
        grad_outs, refs = refs[:4], refs[4:]
        x_s, w_s, dz_s, dx_s, g_s, sems = refs
    else:
        dz_out, refs = refs[0], refs[1:]
        x_s, w_s, dz_s, dx_s, sems = refs
    width, concepts = w_s.shape
    total = n_blocks * cap
    copies = []

    def start(src, dst, n):
        copies.append(pltpu.make_async_copy(src, dst, sems.at[n]))
        copies[-1].start()

    def drain():
        for copy in copies:
            copy.wait()
        copies.clear()

    for i, piece in enumerate(pieces):
        at = 0
        if starts[i] is not None:
            flip, shift = starts[i]
            at = pl.multiple_of((meta_ref[0] ^ flip) * (width // 4) + shift, LANES)
        start(piece, w_s.at[pl.ds(at, piece.shape[0])], i)
    for i, (block, pick) in enumerate(zip(blocks, picks)):
        src = block if pick is None else block.at[pick]
        start(src, x_s.at[pl.ds(i * cap, cap)], n_pieces + i)
    drain()
    for i, block in enumerate(extra[:-1]):
        start(block, x_s.at[pl.ds(total + i * cap, cap)], i)
    if extra:
        start(extra[-1], dz_s.at[pl.ds(total, extra[-1].shape[0])], n_extra)
    later = list(copies)
    copies.clear()
    column = lax.broadcasted_iota(jnp.int32, (cap, concepts), 1)

    @pl.loop(0, n_blocks)
    def _(b):
        here = pl.ds(pl.multiple_of(b * cap, cap), cap)
        z = nn(x_s[here, :width], w_s[...])
        aux = x_s[here, width:].astype(F32)
        weight = aux[:, 0:1]
        label = (aux[:, 1:2] * 32.0 + aux[:, 2:3]).astype(jnp.int32)
        hot = column == label
        top = jnp.max(z, axis=1, keepdims=True)
        exps = jnp.exp(z - top)
        mass = jnp.sum(exps, axis=1, keepdims=True)
        picked = jnp.sum(jnp.where(hot, z, 0.0), axis=1, keepdims=True)
        probs = exps * (1.0 / mass)
        dz = (weight * (probs - jnp.where(hot, 1.0, 0.0))).astype(BF16)
        dz_s[here, :] = dz
        dx_s[here, :width] = nt(dz, w_s[...]).astype(BF16)
        loss = top + jnp.log(mass) - picked
        dx_s[here, width:] = jnp.broadcast_to(loss, (cap, LANES)).astype(BF16)

    for copy in later:
        copy.wait()
    for i, out in enumerate(outs):
        start(dx_s.at[pl.ds(i * cap, cap)], out, i)
    if not with_grads:
        start(dz_s, dz_out, n_blocks)
    else:
        quarter, part = g_s.shape[1], g_s.shape[2]
        for j in range(8):
            at = pl.multiple_of((meta_ref[0] ^ (1, 3, 2, 3, 0, 2, 0, 1)[j]) * quarter, LANES)
            half = (0, 0, 1, 1, 0, 0, 1, 1)[j]
            g_s[j] = tn(
                x_s[:, pl.ds(at, quarter)], dz_s[:, half * part : (half + 1) * part]
            ).astype(BF16)
            if j % 2 == 1:
                start(g_s.at[pl.ds(j - 1, 2)], grad_outs[j // 2], n_blocks + j // 2)
    drain()


def group_step(blocks, pieces, starts, meta, concepts, cap, extra=(), with_grads=True):
    full = blocks[0][0].shape[-1]
    width = full - LANES
    own_rows = cap * len(blocks)
    total = own_rows + cap * max(len(extra) - 1, 0)
    quarter, part = width // 4, concepts // 2
    hbm = pl.BlockSpec(memory_space=pltpu.HBM)
    dx = jax.ShapeDtypeStruct((cap, full), BF16)
    if with_grads:
        rest = [jax.ShapeDtypeStruct((2, quarter, part), BF16)] * 4
        grad_scratch = [pltpu.VMEM((8, quarter, part), BF16)]
    else:
        rest = [jax.ShapeDtypeStruct((total, concepts), BF16)]
        grad_scratch = []
    n_sems = max(len(pieces) + len(blocks), len(blocks) + 4, len(extra) + 1)
    picks = [i for _, i in blocks]
    res = pl.pallas_call(
        lambda *refs: rows_kernel(picks, starts, len(extra), cap, with_grads, *refs),
        in_specs=[pl.BlockSpec(memory_space=pltpu.SMEM)]
        + [pl.BlockSpec(memory_space=pl.ANY)] * (len(blocks) + len(pieces) + len(extra)),
        out_specs=[hbm] * (len(blocks) + len(rest)),
        out_shape=[dx] * len(blocks) + rest,
        scratch_shapes=[
            pltpu.VMEM((total, full), BF16),
            pltpu.VMEM((width, concepts), BF16),
            pltpu.VMEM((total, concepts), BF16),
            pltpu.VMEM((own_rows, full), BF16),
            *grad_scratch,
            pltpu.SemaphoreType.DMA((n_sems,)),
        ],
        compiler_params=pltpu.CompilerParams(vmem_limit_bytes=24 << 20),
        cost_estimate=pl.CostEstimate(
            flops=(4 * own_rows + 2 * total * with_grads) * width * concepts,
            bytes_accessed=4 * (total * full + width * concepts),
            transcendentals=own_rows * concepts,
        ),
    )(meta, *[a for a, _ in blocks], *pieces, *extra)
    return res[: len(blocks)], res[len(blocks) :]


def combine_kernel(n_blocks, cap, key_ref, loss_ref, dz1_ref, w1_ref, *refs):
    blocks, refs = refs[:n_blocks], refs[n_blocks:]
    out_ref, row_loss_ref, x_s, sems = refs

    @pl.when(pl.program_id(0) == 0)
    def _():
        copies = [
            pltpu.make_async_copy(b, x_s.at[pl.ds(i * cap, cap)], sems.at[i])
            for i, b in enumerate(blocks)
        ]
        for copy in copies:
            copy.start()
        for copy in copies:
            copy.wait()

    tile, width = out_ref.shape
    slots = x_s.shape[0]
    place = lax.broadcasted_iota(jnp.int32, (tile, slots), 1)
    pick = jnp.where(upright(key_ref[...]) == place, 1.0, 0.0).astype(BF16)
    got = nn(pick, x_s[...])
    dx1 = tn(dz1_ref[...], w1_ref[...])
    out_ref[...] = (dx1 + got[:, :width]).astype(BF16)
    row_loss_ref[...] = loss_ref[...] + jnp.transpose(got[:, width:])[0:1, :]


def combine(key, loss1, dz1, w1, blocks, cap):
    rows_n = key.shape[1]
    groups_n, width = w1.shape
    full = width + LANES
    tile = cap
    slots = cap * len(blocks)
    line = pl.BlockSpec((1, tile), lambda i: (0, i))
    return pl.pallas_call(
        lambda *refs: combine_kernel(len(blocks), cap, *refs),
        grid=(rows_n // tile,),
        in_specs=[
            line,
            line,
            pl.BlockSpec((groups_n, tile), lambda i: (0, i)),
            pl.BlockSpec((groups_n, width), lambda i: (0, 0)),
        ]
        + [pl.BlockSpec(memory_space=pl.ANY)] * len(blocks),
        out_specs=[pl.BlockSpec((tile, width), lambda i: (i, 0)), line],
        out_shape=[
            jax.ShapeDtypeStruct((rows_n, width), BF16),
            jax.ShapeDtypeStruct((1, rows_n), F32),
        ],
        scratch_shapes=[
            pltpu.VMEM((slots, full), BF16),
            pltpu.SemaphoreType.DMA((len(blocks),)),
        ],
        compiler_params=pltpu.CompilerParams(vmem_limit_bytes=20 << 20),
        cost_estimate=pl.CostEstimate(
            flops=2 * rows_n * slots * full,
            bytes_accessed=2 * (slots * full + rows_n * width),
            transcendentals=0,
        ),
        name="combine",
    )(key, loss1, dz1, w1, *blocks)


def make_local(dp_n, concept_n):
    def pairs(dp_bit, concept_bit):
        return [
            (d * concept_n + c, (d ^ dp_bit) * concept_n + (c ^ concept_bit))
            for d in range(dp_n)
            for c in range(concept_n)
        ]

    core, near, cross, far, away, side, up = (
        pairs(0, 1),
        pairs(0, 2),
        pairs(0, 3),
        pairs(0, 4),
        pairs(0, 6),
        pairs(1, 0),
        pairs(2, 0),
    )

    def send(a, to):
        return lax.ppermute(a, AXES, to)

    def local(embeddings, row_weight, group_label, concept_label, level1_weight, level2_weight):
        return body(
            embeddings, row_weight, group_label, concept_label, level1_weight, level2_weight
        )

    def body(embeddings, row_weight, group_label, concept_label, level1_weight, level2_weight):
        rows_n, width = embeddings.shape
        groups_n = level1_weight.shape[1]
        concepts = level2_weight.shape[2]
        cap = 2 * rows_n // groups_n
        quarter = width // dp_n
        piece = quarter // PIECES
        dp, me = lax.axis_index("dp"), lax.axis_index("concept")

        own = level2_weight[0]

        def spread(q, h):
            qx, qy = send(q, side), send(q, up)
            last = send(qx, up) if h % 2 == 0 else send(qy, side)
            return [q, qx, qy, last]

        pieces2, pieces3, starts = [], [], []
        for h in range(PIECES):
            first = lax.dynamic_slice_in_dim(own, dp * quarter + h * piece, piece, 0)
            far2 = send(first, far)
            far3 = send(far2, near)
            pieces2 += spread(far2, h)
            pieces3 += spread(far3, h)
            starts += [(i, h * piece) for i in range(4)]
        here = dp[None].astype(jnp.int32)

        w1 = level1_weight.T
        groups, weights = group_label.T, row_weight[None, :]
        theirs1, mine1, key, aux = near_rows(
            me[None].astype(jnp.int32),
            groups,
            concept_label[None, :],
            weights,
            embeddings,
            cap,
        )
        rows_in = [send(mine1, near), send(theirs1, cross)]
        theirs, mine, loss1, dz1, grad1 = prepare(key, aux, groups, weights, w1, embeddings, cap)
        got = send(theirs, core)
        for to in (core, side, up, near, far):
            grad1 = grad1 + send(grad1, to)

        whole = [None]

        def step(blocks, pieces, at, **kw):
            return group_step(blocks, pieces, at, here, concepts, cap, **kw)

        dx_1, (dz_in,) = step([(r, None) for r in rows_in], [own], whole, with_grads=False)
        dx_2, grads_2 = step([(mine, 1), (got, 1)], pieces2, starts)
        dx_3, grads_3 = step([(mine, 2), (got, 2)], pieces3, starts)
        dx_0, grads_0 = step([(mine, 0), (got, 0)], [own], whole, extra=(*rows_in, dz_in))

        def scatter(grads):
            to_x, to_y, keep_a, keep_b = (g for g in grads)
            from_x, from_y = send(to_x, side), send(to_y, up)
            pass_a = (keep_a[1].astype(F32) + from_x[1].astype(F32)).astype(BF16)
            pass_b = (keep_b[1].astype(F32) + from_y[1].astype(F32)).astype(BF16)
            last_a = send(pass_a, up)
            last_b = send(pass_b, side)
            sum_a = keep_a[0].astype(F32) + from_x[0].astype(F32) + last_a.astype(F32)
            sum_b = keep_b[0].astype(F32) + from_y[0].astype(F32) + last_b.astype(F32)
            return sum_a, sum_b

        def join(a, b):
            return jnp.concatenate([a, b], axis=1)

        sum2 = join(*scatter(grads_2)).astype(BF16)
        sum3 = join(*scatter(grads_3)).astype(BF16)
        parts0 = scatter(grads_0)
        from2, from3 = send(sum2, far), send(sum3, away)
        level2_grad = (join(*parts0) + from2.astype(F32) + from3.astype(F32)).astype(BF16)[None]

        home = [
            dx_0[0],
            send(dx_0[1], core),
            send(dx_1[0], near),
            send(dx_1[1], cross),
            dx_2[0],
            send(dx_2[1], core),
            dx_3[0],
            send(dx_3[1], core),
        ]
        embed_grad, row_loss = combine(key, loss1, dz1, w1, home, cap)
        return (row_loss[0], embed_grad, grad1.T, level2_grad)

    return local


def solution(mesh):
    dp_n, concept_n = mesh.shape["dp"], mesh.shape["concept"]
    few = dp_n == 4 and concept_n == 8
    return jax.shard_map(
        make_local(dp_n, concept_n) if few else on_device,
        mesh=mesh,
        in_specs=(
            P(("dp", "concept"), None),
            P(("dp", "concept")),
            P(("dp", "concept"), None),
            P(("dp", "concept")),
            P(),
            P("concept", None, None),
        ),
        out_specs=(P(("dp", "concept")), P(("dp", "concept"), None), P(), P("concept", "dp", None)),
        check_vma=False,
    )
```
